32 devices in a mesh: survey: 2 (over x), sub: 8 (over z, y), freq: 2 (over core).
Axes of the slice: x: 2, y: 2, z: 4, core: 2. Of those that a mesh axis runs over, the one named last changes fastest.
Arguments:
- trace_map: bfloat16 [4, 32, 2, 768, 768], P('freq', ('survey', 'sub')), parts along dimension 1, may hold values from -0.109375 to 0.109375
- interior_map: bfloat16 [4, 32, 2, 768, 768], P('freq', ('survey', 'sub')), parts along dimension 1, may hold values from -0.15625 to 0.15625
- excitation: bfloat16 [4, 32, 768, 2, 128], P('freq', ('survey', 'sub')), parts along dimension 1, may hold values from -6 to 6
- receiver_data: bfloat16 [4, 32, 768, 2, 128], P('freq', ('survey', 'sub')), parts along dimension 1, may hold values from -6 to 6
- shot_index: int32 [128], P('survey'), parts along dimension 0, may hold values from 0 to 127, as said below
Outputs:
- image: float32 [32, 768, 768], P(('survey', 'sub'), 'freq'), parts along dimension 0
The draws below stay inside these ranges and needn't reach their ends.
There are 2 independent parts, one for each index of `survey`. The reference program is written for one: setup_inputs(seed, part) draws one part's arguments, and reference() takes and returns one part's arrays. A program takes and returns all parts, laid end to end along the dimension named above; each array names one. Nothing has to cross between parts.
Inputs may be any that keep to these rules, and one draw needn't show every extreme that they name: `shot_index`: 64 distinct shot numbers in shuffled order; 0 and 127 are always among them.
All inputs are finite; a program needn't handle non-finite values.
Results may differ from the reference program's by a relative error of at most 0.0094.
Values may be sent and summed in bfloat16 or wider, within the bound.
A program may use at most 128 MiB of HBM per device.

```python
import jax
import jax.numpy as jnp

K = 768
GY = 4
TICKS = 6
BANK = 128
NS = 64
S = 16
GX = 4
FREQS = 4


def draw_shot_index(key, part):
    first_key = jax.random.fold_in(key, 11)
    second_key = jax.random.fold_in(key, 23)
    middle = 1 + jax.random.permutation(first_key, BANK - 2)[:NS - 2]
    chosen = jnp.concatenate([jnp.array([0, BANK - 1], jnp.int32), middle.astype(jnp.int32)])
    order = jax.random.permutation(second_key, NS)
    return chosen[order].astype(jnp.int32)


def block_scale(stream_key, shape, pieces, least, top_value):
    gain = 1.0
    for position, blocks in pieces:
        steps = jax.random.uniform(jax.random.fold_in(jax.random.fold_in(stream_key, 6), position), (blocks,), jnp.float32, least / len(pieces), top_value / len(pieces))
        gain = gain * jnp.repeat(jnp.exp(steps), shape[position] // blocks).reshape((-1,) + (1,) * (len(shape) - 1 - position))
    return gain


def bell_draw(own_key, dims, scale, limit, split=(), kind=jnp.bfloat16):
    loudness = block_scale(own_key, dims, split, -0.22, 0.18) if split else 1.0
    entries = jax.random.normal(own_key, dims, jnp.float32) * scale * loudness
    return jnp.minimum(jnp.maximum(entries, -limit), limit).astype(kind)


def setup_inputs(seed: int = 0, part: int = 0) -> dict:
    splits = jax.random.split(jax.random.key(seed), 6)
    part_splits = jax.random.split(jax.random.fold_in(splits[5], part), 6)
    return {
        "trace_map": bell_draw(part_splits[0], (FREQS, S, 2, K, K), (4 * K) ** -0.5, 0.109375, ((0, 2), (1, 8))),
        "interior_map": bell_draw(part_splits[1], (FREQS, S, 2, K, K), (2 * K) ** -0.5, 0.15625, ((0, 2), (1, 8))),
        "excitation": bell_draw(part_splits[2], (FREQS, S, K, 2, BANK), 1.0, 6.0, ((0, 2), (1, 8))),
        "receiver_data": bell_draw(part_splits[3], (FREQS, S, K, 2, BANK), 1.0, 6.0, ((0, 2), (1, 8))),
        "shot_index": draw_shot_index(jax.random.fold_in(jax.random.fold_in(splits[5], part), 71), part),
    }


def forward_apply(maps, front):
    values = front.astype(jnp.float32)
    product = jnp.einsum("fsckm,fsmn->fsckn", maps, values)
    real_part = product[:, :, 0, :, :NS] - product[:, :, 1, :, NS:]
    imag_part = product[:, :, 0, :, NS:] + product[:, :, 1, :, :NS]
    return jnp.concatenate([real_part, imag_part], axis=-1)


def adjoint_apply(maps, front):
    values = front.astype(jnp.float32)
    product = jnp.einsum("fsckm,fskn->fscmn", maps, values)
    real_part = product[:, :, 0, :, :NS] + product[:, :, 1, :, NS:]
    imag_part = product[:, :, 0, :, NS:] - product[:, :, 1, :, :NS]
    return jnp.concatenate([real_part, imag_part], axis=-1)


def reference(trace_map, interior_map, excitation, receiver_data, shot_index):
    trace_full = trace_map.astype(jnp.float32)
    interior_full = interior_map.astype(jnp.float32)
    sources = jnp.take(excitation, shot_index, axis=4).reshape(FREQS, S, K, 2 * NS)
    data_front = jnp.take(receiver_data, shot_index, axis=4).reshape(FREQS, S, K, 2 * NS)
    offset = GY + 1
    forward = sources
    adjoint = data_front
    for sweep_step in range(TICKS):
        grid_fwd = jnp.roll(forward, offset, axis=1).reshape(FREQS, GX, GY, K, 2 * NS).astype(jnp.float32)
        left_in = jnp.concatenate([jnp.zeros_like(grid_fwd[:, :, :1]), grid_fwd[:, :, :-1]], axis=2)
        up_in = jnp.concatenate([jnp.zeros_like(grid_fwd[:, :1]), grid_fwd[:, :-1]], axis=1)
        forward_in = jnp.roll((left_in + up_in).astype(jnp.bfloat16).reshape(FREQS, S, K, 2 * NS), -offset, axis=1)
        grid_adj = jnp.roll(adjoint, offset, axis=1).reshape(FREQS, GX, GY, K, 2 * NS).astype(jnp.float32)
        right_in = jnp.concatenate([grid_adj[:, :, 1:], jnp.zeros_like(grid_adj[:, :, :1])], axis=2)
        down_in = jnp.concatenate([grid_adj[:, 1:], jnp.zeros_like(grid_adj[:, :1])], axis=1)
        adjoint_in = jnp.roll((right_in + down_in).astype(jnp.bfloat16).reshape(FREQS, S, K, 2 * NS), -offset, axis=1)
        forward = (sources.astype(jnp.float32) + forward_apply(trace_full, forward_in)).astype(jnp.bfloat16)
        adjoint = (data_front.astype(jnp.float32) + adjoint_apply(trace_full, adjoint_in)).astype(jnp.bfloat16)
    wave = forward_apply(interior_full, forward).astype(jnp.bfloat16)
    back = forward_apply(interior_full, adjoint).astype(jnp.bfloat16)
    scale = (2.0 * NS * FREQS) ** -0.5
    image = jnp.einsum("fsam,fscm->sac", wave.astype(jnp.float32), back.astype(jnp.float32)) * scale
    return image
```

```python
import functools

import jax
import jax.numpy as jnp
from jax import lax
from jax.experimental import pallas as pl
from jax.experimental.pallas import tpu as pltpu
from jax.sharding import PartitionSpec as P

GY = 4
TICKS = 6
PIECES = 4
LATE = 1 << 20
FIRST = (
    (0, 69, 77, 117, 36, 137, 155, 255, 100, 181, 197, 302, 146, 229, 251, 345),
    (295, 197, 176, 118, 256, 139, 117, 64, 201, 74, 59, 27, 111, 42, 36, 0),
)
EVERY = (
    (0, 197, 204, 205, 107, 419, 422, 312, 214, 413, 423, 303, 210, 416, 413, 320),
    (399, 442, 440, 257, 399, 434, 434, 261, 387, 408, 394, 172, 408, 120, 120, 0),
)
COLS = 256
MESH = pl.DeviceIdType.MESH
NT = (((1,), (1,)), ((), ()))
NN = (((1,), (0,)), ((), ()))
TN = (((0,), (0,)), ((), ()))


def dot(a, b, dims):
    return lax.dot_general(a, b, dims, preferred_element_type=jnp.float32)


def sweep(
    count,
    freqs,
    subs,
    scale,
    trace_hbm,
    interior_hbm,
    src_ref,
    image_ref,
    trace,
    interior,
    val,
    recv,
    xin,
    wave,
    back,
    wave_in,
    back_in,
    load_sem,
    send_sem,
    recv_sem,
    hand_sem,
    swap_send,
    swap_recv,
):
    total = count * subs
    rows = total // GY
    deepest = rows - 1 + GY - 1
    spare = max(0, deepest - TICKS)
    reach = GY // subs
    chunks = freqs * PIECES
    width = src_ref.shape[-1]
    tall = src_ref.shape[-2]
    half = tall // 2
    me = lax.axis_index("sub")
    q = lax.axis_index("freq")
    other = 1 - q

    loads = []
    for m, (hbm, vmem) in enumerate(((trace_hbm, trace), (interior_hbm, interior))):
        for f in range(freqs):
            for l in range(subs):
                loads.append(
                    pltpu.make_async_copy(hbm.at[f, l], vmem.at[f, l], load_sem.at[m, f, l])
                )
    for load in loads:
        load.start()

    barrier = pltpu.get_barrier_semaphore()
    for by in (1, count - 1, reach, count - reach):
        pl.semaphore_signal(
            barrier, inc=1, device_id={"sub": lax.rem(me + by, count)}, device_id_type=MESH
        )
    pl.semaphore_signal(barrier, inc=1, device_id={"freq": other}, device_id_type=MESH)
    pl.semaphore_wait(barrier, 5)

    def place(l):
        g = lax.rem(me * subs + l + GY + 1, total)
        return g // GY, lax.rem(g, GY)

    def depth(l, way):
        r, c = place(l)
        return r + c if way == 0 else deepest - r - c

    def copy_of(ref, way, slot, v, ch, by, part=slice(None), sem=None):
        return pltpu.make_async_remote_copy(
            src_ref=ref.at[:, part],
            dst_ref=recv.at[way, slot, v, ch, :, part],
            send_sem=send_sem.at[way, slot, v, ch] if sem is None else sem,
            recv_sem=recv_sem.at[way, slot, v, ch],
            device_id={"sub": lax.rem(me + (by if way == 0 else count - by), count)},
            device_id_type=MESH,
        )

    def edges(l, way):
        r, c = place(l)
        if way == 0:
            return r > 0, c > 0, r < rows - 1, c < GY - 1, l == 0, l == subs - 1, l - 1
        return r < rows - 1, c < GY - 1, r > 0, c > 0, l == subs - 1, l == 0, l + 1

    relays = reach == 2 and count % 2 == 0
    parity = lax.rem(me, 2)

    def both(*flags):
        return functools.reduce(jnp.logical_and, flags)

    def send(ref, l, way, v, ch, part=slice(None)):
        _, _, below, aside, _, far_out, _ = edges(l, way)

        @pl.when(below)
        def _():
            copy_of(ref, way, 1 + l, v, ch, reach, part).start()

        if far_out:

            @pl.when(direct(way, aside, below))
            def _():
                copy_of(ref, way, 0, v, ch, 1, part).start()

    def direct(way, aside, below):
        if not relays:
            return aside
        return both(aside, jnp.logical_not(both(parity == 1 - way, below)))

    def handed(l, way):
        above, _, _, _, _, far_out, _ = edges(l, way)
        return both(parity == 1 - way, above) if relays and far_out else None

    def hand_on(way, l, v, ch):
        return copy_of(
            recv.at[way, 1 + l, v, ch], way, 0, v, ch, count - 1, sem=hand_sem.at[way, v, ch]
        )

    def each(body):
        if spare == 0:
            lax.fori_loop(0, chunks, lambda ch, _: (body(0, ch), 0)[1], 0)
        else:

            def outer(v, _):
                lax.fori_loop(0, chunks, lambda ch, _: (body(v, ch), 0)[1], 0)
                return 0

            lax.fori_loop(0, spare + 1, outer, 0)

    def first(v, ch):
        for l in range(subs):
            for way in range(2):

                @pl.when(depth(l, way) == v)
                def _():
                    send(src_ref.at[way, l, ch], l, way, v, ch)
                    val[way, l, v, ch] = src_ref[way, l, ch]

    each(first)
    for load in loads[: freqs * subs]:
        load.wait()

    def step(t, v, ch, l, way):
        f = ch // PIECES
        above, beside, _, _, far_in, _, near = edges(l, way)

        @pl.when(above)
        def _():
            copy_of(val.at[way, l, v, ch], way, 1 + l, v, ch, reach).wait_recv()
            hands = handed(l, way)
            if hands is not None:

                @pl.when(hands)
                def _():
                    hand_on(way, l, v, ch).start()

            xin[...] = recv[way, 1 + l, v, ch]

        @pl.when(jnp.logical_not(above))
        def _():
            xin[...] = jnp.zeros_like(xin)

        @pl.when(beside)
        def _():
            if far_in:
                copy_of(val.at[way, l, v, ch], way, 0, v, ch, 1).wait_recv()
                side = recv[way, 0, v, ch]
            else:
                side = val[way, near, v, ch]
            xin[...] = (xin[...].astype(jnp.float32) + side.astype(jnp.float32)).astype(
                jnp.bfloat16
            )

        x = xin[...]
        for n in range(0, width, COLS):
            span = slice(n, n + COLS)
            if way == 0:
                p = dot(x, trace[f, l, 0, span, :], NT)
                s = dot(x, trace[f, l, 1, span, :], NT)
                real, imag = p[:half] - s[half:], p[half:] + s[:half]
            else:
                p = dot(x, trace[f, l, 0, :, span], NN)
                s = dot(x, trace[f, l, 1, :, span], NN)
                real, imag = p[:half] + s[half:], p[half:] - s[:half]
            mine = src_ref[way, l, ch, :, span].astype(jnp.float32)
            val[way, l, v, ch, :half, span] = (mine[:half] + real).astype(jnp.bfloat16)
            val[way, l, v, ch, half:, span] = (mine[half:] + imag).astype(jnp.bfloat16)

            @pl.when(t < TICKS)
            def _():
                send(val.at[way, l, v, ch], l, way, v, ch, span)

    kinds = []
    for l in range(subs):
        for way in range(2):
            r, c = place(l)
            for v in range(spare + 1):
                t = depth(l, way) - v
                begin, pace = 60 * t, 300
                if (count, total, spare) == (8, 16, 0):
                    for g in range(total):
                        here = r * GY + c == g
                        begin = jnp.where(here, FIRST[way][g], begin)
                        pace = jnp.where(here, EVERY[way][g], pace)
                kinds.append((l, way, v, t, both(t >= 1, t <= TICKS), begin * 10, pace))
    jobs = chunks * sum(valid.astype(jnp.int32) for *_, valid, _, _ in kinds)

    def turn(_, done):
        due = [
            jnp.where(both(valid, n < chunks), begin + pace * n, LATE)
            for n, (*_, valid, begin, pace) in zip(done, kinds)
        ]
        least = functools.reduce(jnp.minimum, due)
        free = jnp.bool_(True)
        after = []
        for n, time, (l, way, v, t, *_) in zip(done, due, kinds):
            mine = both(free, time == least)
            free = both(free, jnp.logical_not(mine))

            @pl.when(mine)
            def _():
                step(t, v, n, l, way)

            after.append(n + mine.astype(jnp.int32))
        return tuple(after)

    lax.fori_loop(0, jobs, turn, tuple(jnp.int32(0) for _ in kinds))

    for load in loads[freqs * subs :]:
        load.wait()

    width_half = width // 2
    keep = pl.ds(pl.multiple_of(q * width_half, width_half), width_half)
    give = pl.ds(pl.multiple_of(other * width_half, width_half), width_half)
    swaps = {}
    for l in range(subs):
        for f in range(freqs):
            stack = []
            for way in range(2):
                v = 0 if spare == 0 else jnp.maximum(depth(l, way) - TICKS, 0)
                for piece in range(PIECES):
                    stack.append(val[way, l, v, f * PIECES + piece])
            x = jnp.concatenate(stack, axis=0)
            high = x.shape[0] // 2
            for n in range(0, width, COLS):
                span = slice(n, n + COLS)
                p = dot(x, interior[f, l, 0, span, :], NT)
                s = dot(x, interior[f, l, 1, span, :], NT)
                p = p.reshape(-1, 2, half, COLS)
                s = s.reshape(-1, 2, half, COLS)
                y = jnp.stack([p[:, 0] - s[:, 1], p[:, 1] + s[:, 0]], axis=1)
                y = y.reshape(2, high, COLS).astype(jnp.bfloat16)
                wave[l, f, :, span] = y[0]
                back[l, f, :, span] = y[1]
            for k, (src, dst) in enumerate(
                ((wave.at[l, f, :, give], wave_in.at[l, f]), (back.at[l, f], back_in.at[l, f]))
            ):
                swap = pltpu.make_async_remote_copy(
                    src_ref=src,
                    dst_ref=dst,
                    send_sem=swap_send.at[k, l, f],
                    recv_sem=swap_recv.at[k, l, f],
                    device_id={"freq": other},
                    device_id_type=MESH,
                )
                swap.start()
                swaps[k, l, f] = swap
    for l in range(subs):
        for f in range(freqs):
            swaps[0, l, f].wait_recv()
            swaps[1, l, f].wait_recv()
        left = [wave[l, f, :, keep] for f in range(freqs)] + [wave_in[l, f] for f in range(freqs)]
        left = jnp.concatenate(left, axis=0)
        for n in range(0, width, COLS):
            span = slice(n, n + COLS)
            right = [back[l, f, :, span] for f in range(freqs)]
            right += [back_in[l, f, :, span] for f in range(freqs)]
            image_ref[l, :, span] = dot(left, jnp.concatenate(right, axis=0), TN) * scale
    for swap in swaps.values():
        swap.wait_send()

    def finish(v, ch):
        for l in range(subs):
            for way in range(2):
                here = depth(l, way)
                _, _, below, aside, _, far_out, _ = edges(l, way)
                sent = jnp.logical_and(here >= v, here < v + TICKS)
                if far_out:

                    @pl.when(both(sent, direct(way, aside, below)))
                    def _():
                        copy_of(val.at[way, l, v, ch], way, 0, v, ch, 1).wait_send()

                hands = handed(l, way)
                if hands is not None:

                    @pl.when(both(hands, here - v >= 1, here - v <= TICKS))
                    def _():
                        hand_on(way, l, v, ch).wait_send()

                @pl.when(jnp.logical_and(sent, below))
                def _():
                    copy_of(val.at[way, l, v, ch], way, 1 + l, v, ch, reach).wait_send()

    each(finish)


def per_device(trace_map, interior_map, excitation, receiver_data, shot_index):
    freqs, subs, _, width, _ = trace_map.shape
    shots = shot_index.shape[0]
    bank = excitation.shape[4]
    count = lax.axis_size("sub")
    half = shots // PIECES
    chunks = freqs * PIECES
    chooser = (
        lax.broadcasted_iota(jnp.int32, (shots, bank), 1) == shot_index[:, None]
    ).astype(jnp.bfloat16).reshape(PIECES, half, bank)

    def pick(table):
        picked = jnp.einsum("fsxcb,pnb->sfpcnx", table, chooser, preferred_element_type=jnp.float32)
        return picked.astype(jnp.bfloat16).reshape(subs, chunks, 2 * half, width)

    src = jnp.stack([pick(excitation), pick(receiver_data)])
    rows = count * subs // GY
    spare = max(0, rows + GY - 2 - TICKS)
    scale = (2.0 * shots * freqs * lax.axis_size("freq")) ** (-0.5)
    bf = jnp.bfloat16
    dma = pltpu.SemaphoreType.DMA
    front = (chunks, 2 * half, width)
    return pl.pallas_call(
        functools.partial(sweep, count, freqs, subs, scale),
        out_shape=jax.ShapeDtypeStruct((subs, width // 2, width), jnp.float32),
        in_specs=[
            pl.BlockSpec(memory_space=pl.ANY),
            pl.BlockSpec(memory_space=pl.ANY),
            pl.BlockSpec(memory_space=pltpu.VMEM),
        ],
        out_specs=pl.BlockSpec(memory_space=pltpu.VMEM),
        scratch_shapes=[
            pltpu.VMEM(trace_map.shape, bf),
            pltpu.VMEM(interior_map.shape, bf),
            pltpu.VMEM((2, subs, spare + 1) + front, bf),
            pltpu.VMEM((2, subs + 1, spare + 1) + front, bf),
            pltpu.VMEM((2 * half, width), bf),
            pltpu.VMEM((subs, freqs, 2 * shots, width), bf),
            pltpu.VMEM((subs, freqs, 2 * shots, width), bf),
            pltpu.VMEM((subs, freqs, 2 * shots, width // 2), bf),
            pltpu.VMEM((subs, freqs, 2 * shots, width), bf),
            dma((2, freqs, subs)),
            dma((2, subs + 1, spare + 1, chunks)),
            dma((2, subs + 1, spare + 1, chunks)),
            dma((2, spare + 1, chunks)),
            dma((2, subs, freqs)),
            dma((2, subs, freqs)),
        ],
        compiler_params=pltpu.CompilerParams(
            collective_id=0, has_side_effects=True, vmem_limit_bytes=60 * 1024 * 1024
        ),
    )(trace_map, interior_map, src)


def solution(mesh):
    placed = (
        P("freq", ("survey", "sub"), None, None, None),
        P("freq", ("survey", "sub"), None, None, None),
        P("freq", ("survey", "sub"), None, None, None),
        P("freq", ("survey", "sub"), None, None, None),
        P("survey"),
    )
    return jax.shard_map(
        per_device,
        mesh=mesh,
        in_specs=placed,
        out_specs=P(("survey", "sub"), "freq", None),
        check_vma=False,
    )
```

```python
import functools

import jax
import jax.numpy as jnp
from jax import lax
from jax.experimental import pallas as pl
from jax.experimental.pallas import tpu as pltpu
from jax.sharding import PartitionSpec as P

GY = 4
TICKS = 6
PIECES = 4
VMEM = 60 << 20
LATE = 1 << 20
FIRST = (
    (0, 69, 77, 117, 36, 137, 155, 255, 100, 181, 197, 302, 146, 229, 251, 345),
    (295, 197, 176, 118, 256, 139, 117, 64, 201, 74, 59, 27, 111, 42, 36, 0),
)
EVERY = (
    (0, 197, 204, 205, 107, 419, 422, 312, 214, 413, 423, 303, 210, 416, 413, 320),
    (399, 442, 440, 257, 399, 434, 434, 261, 387, 408, 394, 172, 408, 120, 120, 0),
)
COLS = 256
MESH = pl.DeviceIdType.MESH
NT = (((1,), (1,)), ((), ()))
NN = (((1,), (0,)), ((), ()))
TN = (((0,), (0,)), ((), ()))


def dot(a, b, dims):
    return lax.dot_general(a, b, dims, preferred_element_type=jnp.float32)


def sweep(
    count,
    freqs,
    subs,
    trace_hbm,
    interior_hbm,
    fired_hbm,
    heard_hbm,
    shot_ref,
    image_ref,
    trace,
    interior,
    bank,
    plain,
    src_ref,
    val,
    recv,
    xin,
    wave,
    back,
    wave_in,
    back_in,
    load_sem,
    bank_sem,
    send_sem,
    recv_sem,
    hand_sem,
    swap_send,
    swap_recv,
):
    total = count * subs
    rows = total // GY
    deepest = rows - 1 + GY - 1
    spare = max(0, deepest - TICKS)
    reach = GY // subs
    chunks = freqs * PIECES
    width = val.shape[-1]
    tall = val.shape[-2]
    half = tall // 2
    me = lax.axis_index("sub")
    q = lax.axis_index("freq")
    other = 1 - q

    def bank_load(way, l, f):
        hbm = (fired_hbm, heard_hbm)[way]
        return pltpu.make_async_copy(hbm.at[f, l], bank.at[way, l, f], bank_sem.at[way, l, f])

    def map_load(m, f, l):
        hbm, vmem = ((trace_hbm, trace), (interior_hbm, interior))[m]
        return pltpu.make_async_copy(hbm.at[f, l], vmem.at[f, l], load_sem.at[m, f, l])

    every = [(f, l) for f in range(freqs) for l in range(subs)]
    for f, l in every:
        for way in range(2):
            bank_load(way, l, f).start()
    for f, l in every:
        map_load(0, f, l).start()

    barrier = pltpu.get_barrier_semaphore()
    for by in (1, count - 1, reach, count - reach):
        pl.semaphore_signal(
            barrier, inc=1, device_id={"sub": lax.rem(me + by, count)}, device_id_type=MESH
        )
    pl.semaphore_signal(barrier, inc=1, device_id={"freq": other}, device_id_type=MESH)

    def place(l):
        g = lax.rem(me * subs + l + GY + 1, total)
        return g // GY, lax.rem(g, GY)

    def depth(l, way):
        r, c = place(l)
        return r + c if way == 0 else deepest - r - c

    def copy_of(ref, way, slot, v, ch, by, sem=None):
        return pltpu.make_async_remote_copy(
            src_ref=ref,
            dst_ref=recv.at[way, slot, v, ch],
            send_sem=send_sem.at[way, slot, v, ch] if sem is None else sem,
            recv_sem=recv_sem.at[way, slot, v, ch],
            device_id={"sub": lax.rem(me + (by if way == 0 else count - by), count)},
            device_id_type=MESH,
        )

    def edges(l, way):
        r, c = place(l)
        if way == 0:
            return r > 0, c > 0, r < rows - 1, c < GY - 1, l == 0, l == subs - 1, l - 1
        return r < rows - 1, c < GY - 1, r > 0, c > 0, l == subs - 1, l == 0, l + 1

    relays = reach == 2 and count % 2 == 0
    parity = lax.rem(me, 2)

    def both(*flags):
        return functools.reduce(jnp.logical_and, flags)

    def send(ref, l, way, v, ch):
        _, _, below, aside, _, far_out, _ = edges(l, way)

        @pl.when(below)
        def _():
            copy_of(ref, way, 1 + l, v, ch, reach).start()

        if far_out:

            @pl.when(direct(way, aside, below))
            def _():
                copy_of(ref, way, 0, v, ch, 1).start()

    def direct(way, aside, below):
        if not relays:
            return aside
        return both(aside, jnp.logical_not(both(parity == 1 - way, below)))

    def handed(l, way):
        above, _, _, _, _, far_out, _ = edges(l, way)
        return both(parity == 1 - way, above) if relays and far_out else None

    def hand_on(way, l, v, ch):
        return copy_of(
            recv.at[way, 1 + l, v, ch], way, 0, v, ch, count - 1, sem=hand_sem.at[way, v, ch]
        )

    def each(body):
        if spare == 0:
            lax.fori_loop(0, chunks, lambda ch, _: (body(0, ch), 0)[1], 0)
        else:

            def outer(v, _):
                lax.fori_loop(0, chunks, lambda ch, _: (body(v, ch), 0)[1], 0)
                return 0

            lax.fori_loop(0, spare + 1, outer, 0)

    shots = shot_ref.shape[1]
    number = lax.broadcasted_iota(jnp.int32, (bank.shape[-1], shots), 0)
    chooser = jnp.transpose((number == shot_ref[...]).astype(jnp.float32)).astype(jnp.bfloat16)

    def pick(way, l, f):
        bank_load(way, l, f).wait()
        plain[...] = bank[way, l, f].astype(jnp.float32)
        for c in range(2):
            rows_of = plain[pl.ds(c, width, stride=2), :].astype(jnp.bfloat16)
            picked = dot(chooser, rows_of, NT).astype(jnp.bfloat16)
            for piece in range(PIECES):
                src_ref[way, l, f * PIECES + piece, c * half : (c + 1) * half, :] = picked[
                    piece * half : (piece + 1) * half
                ]

    def pick_all(early):
        for l in range(subs):
            for way in range(2):

                @pl.when((depth(l, way) <= spare) == early)
                def _():
                    lax.fori_loop(0, freqs, lambda f, _: (pick(way, l, f), 0)[1], 0)

    def first(v, ch):
        for l in range(subs):
            for way in range(2):

                @pl.when(depth(l, way) == v)
                def _():
                    send(src_ref.at[way, l, ch], l, way, v, ch)
                    val[way, l, v, ch] = src_ref[way, l, ch]

    pick_all(True)
    pl.semaphore_wait(barrier, 5)
    each(first)
    pick_all(False)
    for f, l in every:
        map_load(0, f, l).wait()
    for f, l in every:
        map_load(1, f, l).start()

    def step(t, v, ch, l, way):
        f = ch // PIECES
        above, beside, _, _, far_in, _, near = edges(l, way)

        @pl.when(above)
        def _():
            copy_of(val.at[way, l, v, ch], way, 1 + l, v, ch, reach).wait_recv()
            hands = handed(l, way)
            if hands is not None:

                @pl.when(hands)
                def _():
                    hand_on(way, l, v, ch).start()

            xin[...] = recv[way, 1 + l, v, ch]

        @pl.when(jnp.logical_not(above))
        def _():
            xin[...] = jnp.zeros_like(xin)

        @pl.when(beside)
        def _():
            if far_in:
                copy_of(val.at[way, l, v, ch], way, 0, v, ch, 1).wait_recv()
                side = recv[way, 0, v, ch]
            else:
                side = val[way, near, v, ch]
            xin[...] = (xin[...].astype(jnp.float32) + side.astype(jnp.float32)).astype(
                jnp.bfloat16
            )

        x = xin[...]
        for n in range(0, width, COLS):
            span = slice(n, n + COLS)
            if way == 0:
                p = dot(x, trace[f, l, 0, span, :], NT)
                s = dot(x, trace[f, l, 1, span, :], NT)
                real, imag = p[:half] - s[half:], p[half:] + s[:half]
            else:
                p = dot(x, trace[f, l, 0, :, span], NN)
                s = dot(x, trace[f, l, 1, :, span], NN)
                real, imag = p[:half] + s[half:], p[half:] - s[:half]
            mine = src_ref[way, l, ch, :, span].astype(jnp.float32)
            val[way, l, v, ch, :half, span] = (mine[:half] + real).astype(jnp.bfloat16)
            val[way, l, v, ch, half:, span] = (mine[half:] + imag).astype(jnp.bfloat16)

        @pl.when(t < TICKS)
        def _():
            send(val.at[way, l, v, ch], l, way, v, ch)

    kinds = []
    for l in range(subs):
        for way in range(2):
            r, c = place(l)
            for v in range(spare + 1):
                t = depth(l, way) - v
                begin, pace = 60 * t, 300
                if (count, total, spare) == (8, 16, 0):
                    for g in range(total):
                        here = r * GY + c == g
                        begin = jnp.where(here, FIRST[way][g], begin)
                        pace = jnp.where(here, EVERY[way][g], pace)
                kinds.append((l, way, v, t, both(t >= 1, t <= TICKS), begin * 10, pace))
    jobs = chunks * sum(valid.astype(jnp.int32) for *_, valid, _, _ in kinds)

    def turn(_, done):
        due = [
            jnp.where(both(valid, n < chunks), begin + pace * n, LATE)
            for n, (*_, valid, begin, pace) in zip(done, kinds)
        ]
        least = functools.reduce(jnp.minimum, due)
        free = jnp.bool_(True)
        after = []
        for n, time, (l, way, v, t, *_) in zip(done, due, kinds):
            mine = both(free, time == least)
            free = both(free, jnp.logical_not(mine))

            @pl.when(mine)
            def _():
                step(t, v, n, l, way)

            after.append(n + mine.astype(jnp.int32))
        return tuple(after)

    lax.fori_loop(0, jobs, turn, tuple(jnp.int32(0) for _ in kinds))

    for f, l in every:
        map_load(1, f, l).wait()

    width_half = width // 2
    keep = pl.ds(pl.multiple_of(q * width_half, width_half), width_half)
    give = pl.ds(pl.multiple_of(other * width_half, width_half), width_half)
    swaps = {}
    for l in range(subs):
        for f in range(freqs):
            stack = []
            for way in range(2):
                v = 0 if spare == 0 else jnp.maximum(depth(l, way) - TICKS, 0)
                for piece in range(PIECES):
                    stack.append(val[way, l, v, f * PIECES + piece])
            x = jnp.concatenate(stack, axis=0)
            high = x.shape[0] // 2
            for n in range(0, width, COLS):
                span = slice(n, n + COLS)
                p = dot(x, interior[f, l, 0, span, :], NT)
                s = dot(x, interior[f, l, 1, span, :], NT)
                p = p.reshape(-1, 2, half, COLS)
                s = s.reshape(-1, 2, half, COLS)
                y = jnp.stack([p[:, 0] - s[:, 1], p[:, 1] + s[:, 0]], axis=1)
                y = y.reshape(2, high, COLS).astype(jnp.bfloat16)
                wave[l, f, :, span] = y[0]
                back[l, f, :, span] = y[1]
            for k, (src, dst) in enumerate(
                ((wave.at[l, f, :, give], wave_in.at[l, f]), (back.at[l, f], back_in.at[l, f]))
            ):
                swap = pltpu.make_async_remote_copy(
                    src_ref=src,
                    dst_ref=dst,
                    send_sem=swap_send.at[k, l, f],
                    recv_sem=swap_recv.at[k, l, f],
                    device_id={"freq": other},
                    device_id_type=MESH,
                )
                swap.start()
                swaps[k, l, f] = swap
    for l in range(subs):
        for f in range(freqs):
            swaps[0, l, f].wait_recv()
            swaps[1, l, f].wait_recv()
        left = [wave[l, f, :, keep] for f in range(freqs)] + [wave_in[l, f] for f in range(freqs)]
        left = jnp.concatenate(left, axis=0)
        for n in range(0, width, COLS):
            span = slice(n, n + COLS)
            right = [back[l, f, :, span] for f in range(freqs)]
            right += [back_in[l, f, :, span] for f in range(freqs)]
            image_ref[l, :, span] = dot(left, jnp.concatenate(right, axis=0), TN)
    for swap in swaps.values():
        swap.wait_send()

    def finish(v, ch):
        for l in range(subs):
            for way in range(2):
                here = depth(l, way)
                _, _, below, aside, _, far_out, _ = edges(l, way)
                sent = jnp.logical_and(here >= v, here < v + TICKS)
                if far_out:

                    @pl.when(both(sent, direct(way, aside, below)))
                    def _():
                        copy_of(val.at[way, l, v, ch], way, 0, v, ch, 1).wait_send()

                hands = handed(l, way)
                if hands is not None:

                    @pl.when(both(hands, here - v >= 1, here - v <= TICKS))
                    def _():
                        hand_on(way, l, v, ch).wait_send()

                @pl.when(jnp.logical_and(sent, below))
                def _():
                    copy_of(val.at[way, l, v, ch], way, 1 + l, v, ch, reach).wait_send()

    each(finish)


def per_device(trace_map, interior_map, excitation, receiver_data, shot_index):
    freqs, subs, _, width, _ = trace_map.shape
    shots = shot_index.shape[0]
    bank = excitation.shape[4]
    count = lax.axis_size("sub")
    half = shots // PIECES
    chunks = freqs * PIECES
    rows = count * subs // GY
    spare = max(0, rows + GY - 2 - TICKS)
    scale = (2.0 * shots * freqs * lax.axis_size("freq")) ** (-0.5)
    bf = jnp.bfloat16
    flat = (freqs, subs, 2 * width, bank)
    dma = pltpu.SemaphoreType.DMA
    front = (chunks, 2 * half, width)
    image = pl.pallas_call(
        functools.partial(sweep, count, freqs, subs),
        out_shape=jax.ShapeDtypeStruct((subs, width // 2, width), jnp.float32),
        in_specs=[
            pl.BlockSpec(memory_space=pl.ANY),
            pl.BlockSpec(memory_space=pl.ANY),
            pl.BlockSpec(memory_space=pl.ANY),
            pl.BlockSpec(memory_space=pl.ANY),
            pl.BlockSpec(memory_space=pltpu.VMEM),
        ],
        out_specs=pl.BlockSpec(memory_space=pltpu.VMEM),
        scratch_shapes=[
            pltpu.VMEM(trace_map.shape, bf),
            pltpu.VMEM(interior_map.shape, bf),
            pltpu.VMEM((2, subs, freqs, 2 * width, bank), bf),
            pltpu.VMEM((2 * width, bank), jnp.float32),
            pltpu.VMEM((2, subs) + front, bf),
            pltpu.VMEM((2, subs, spare + 1) + front, bf),
            pltpu.VMEM((2, subs + 1, spare + 1) + front, bf),
            pltpu.VMEM((2 * half, width), bf),
            pltpu.VMEM((subs, freqs, 2 * shots, width), bf),
            pltpu.VMEM((subs, freqs, 2 * shots, width), bf),
            pltpu.VMEM((subs, freqs, 2 * shots, width // 2), bf),
            pltpu.VMEM((subs, freqs, 2 * shots, width), bf),
            dma((2, freqs, subs)),
            dma((2, subs, freqs)),
            dma((2, subs + 1, spare + 1, chunks)),
            dma((2, subs + 1, spare + 1, chunks)),
            dma((2, spare + 1, chunks)),
            dma((2, subs, freqs)),
            dma((2, subs, freqs)),
        ],
        compiler_params=pltpu.CompilerParams(
            collective_id=0, has_side_effects=True, vmem_limit_bytes=VMEM
        ),
    )(
        trace_map,
        interior_map,
        excitation.reshape(flat),
        receiver_data.reshape(flat),
        shot_index.reshape(1, shots),
    )
    return image * scale


def solution(mesh):
    placed = (
        P("freq", ("survey", "sub"), None, None, None),
        P("freq", ("survey", "sub"), None, None, None),
        P("freq", ("survey", "sub"), None, None, None),
        P("freq", ("survey", "sub"), None, None, None),
        P("survey"),
    )
    return jax.shard_map(
        per_device,
        mesh=mesh,
        in_specs=placed,
        out_specs=P(("survey", "sub"), "freq", None),
        check_vma=False,
    )
```

```python
import functools

import jax
import jax.numpy as jnp
from jax import lax
from jax.experimental import pallas as pl
from jax.experimental.pallas import tpu as pltpu
from jax.sharding import PartitionSpec as P

GY = 4
TICKS = 6
PIECES = 4
VMEM = 58 << 20
LATE = 1 << 20
FIRST = (
    (0, 69, 77, 117, 36, 137, 155, 255, 100, 181, 197, 302, 146, 229, 251, 345),
    (295, 197, 176, 118, 256, 139, 117, 64, 201, 74, 59, 27, 111, 42, 36, 0),
)
EVERY = (
    (0, 197, 204, 205, 107, 419, 422, 312, 214, 413, 423, 303, 210, 416, 413, 320),
    (399, 442, 440, 257, 399, 434, 434, 261, 387, 408, 394, 172, 408, 120, 120, 0),
)
COLS = 256
MESH = pl.DeviceIdType.MESH
NT = (((1,), (1,)), ((), ()))
NN = (((1,), (0,)), ((), ()))


def dot(a, b, dims):
    return lax.dot_general(a, b, dims, preferred_element_type=jnp.float32)


def sweep(
    count,
    freqs,
    subs,
    trace_hbm,
    interior_hbm,
    fired_hbm,
    heard_hbm,
    shot_ref,
    left_hbm,
    right_hbm,
    trace,
    interior,
    bank,
    plain,
    src_ref,
    val,
    recv,
    xin,
    wave,
    back,
    load_sem,
    bank_sem,
    send_sem,
    recv_sem,
    hand_sem,
    swap_send,
    swap_recv,
    keep_sem,
):
    total = count * subs
    rows = total // GY
    deepest = rows - 1 + GY - 1
    spare = max(0, deepest - TICKS)
    reach = GY // subs
    chunks = freqs * PIECES
    width = val.shape[-1]
    tall = val.shape[-2]
    half = tall // 2
    me = lax.axis_index("sub")
    q = lax.axis_index("freq")
    other = 1 - q

    def bank_load(way, l, f):
        hbm = (fired_hbm, heard_hbm)[way]
        return pltpu.make_async_copy(hbm.at[f, l], bank.at[way, l, f], bank_sem.at[way, l, f])

    def map_load(m, f, l):
        hbm, vmem = ((trace_hbm, trace), (interior_hbm, interior))[m]
        return pltpu.make_async_copy(hbm.at[f, l], vmem.at[f, l], load_sem.at[m, f, l])

    every = [(f, l) for f in range(freqs) for l in range(subs)]
    for f, l in every:
        for way in range(2):
            bank_load(way, l, f).start()
    for f, l in every:
        map_load(0, f, l).start()

    barrier = pltpu.get_barrier_semaphore()
    for by in (1, count - 1, reach, count - reach):
        pl.semaphore_signal(
            barrier, inc=1, device_id={"sub": lax.rem(me + by, count)}, device_id_type=MESH
        )
    pl.semaphore_signal(barrier, inc=1, device_id={"freq": other}, device_id_type=MESH)

    def place(l):
        g = lax.rem(me * subs + l + GY + 1, total)
        return g // GY, lax.rem(g, GY)

    def depth(l, way):
        r, c = place(l)
        return r + c if way == 0 else deepest - r - c

    def copy_of(ref, way, slot, v, ch, by, sem=None):
        return pltpu.make_async_remote_copy(
            src_ref=ref,
            dst_ref=recv.at[way, slot, v, ch],
            send_sem=send_sem.at[way, slot, v, ch] if sem is None else sem,
            recv_sem=recv_sem.at[way, slot, v, ch],
            device_id={"sub": lax.rem(me + (by if way == 0 else count - by), count)},
            device_id_type=MESH,
        )

    def edges(l, way):
        r, c = place(l)
        if way == 0:
            return r > 0, c > 0, r < rows - 1, c < GY - 1, l == 0, l == subs - 1, l - 1
        return r < rows - 1, c < GY - 1, r > 0, c > 0, l == subs - 1, l == 0, l + 1

    relays = reach == 2 and count % 2 == 0
    parity = lax.rem(me, 2)

    def both(*flags):
        return functools.reduce(jnp.logical_and, flags)

    def send(ref, l, way, v, ch):
        _, _, below, aside, _, far_out, _ = edges(l, way)

        @pl.when(below)
        def _():
            copy_of(ref, way, 1 + l, v, ch, reach).start()

        if far_out:

            @pl.when(direct(way, aside, below))
            def _():
                copy_of(ref, way, 0, v, ch, 1).start()

    def direct(way, aside, below):
        if not relays:
            return aside
        return both(aside, jnp.logical_not(both(parity == 1 - way, below)))

    def handed(l, way):
        above, _, _, _, _, far_out, _ = edges(l, way)
        return both(parity == 1 - way, above) if relays and far_out else None

    def hand_on(way, l, v, ch):
        return copy_of(
            recv.at[way, 1 + l, v, ch], way, 0, v, ch, count - 1, sem=hand_sem.at[way, v, ch]
        )

    def each(body):
        if spare == 0:
            lax.fori_loop(0, chunks, lambda ch, _: (body(0, ch), 0)[1], 0)
        else:

            def outer(v, _):
                lax.fori_loop(0, chunks, lambda ch, _: (body(v, ch), 0)[1], 0)
                return 0

            lax.fori_loop(0, spare + 1, outer, 0)

    shots = shot_ref.shape[1]
    number = lax.broadcasted_iota(jnp.int32, (bank.shape[-1], shots), 0)
    chooser = jnp.transpose((number == shot_ref[...]).astype(jnp.float32)).astype(jnp.bfloat16)

    def pick(way, l, f):
        bank_load(way, l, f).wait()
        plain[...] = bank[way, l, f].astype(jnp.float32)
        for c in range(2):
            rows_of = plain[pl.ds(c, width, stride=2), :].astype(jnp.bfloat16)
            picked = dot(chooser, rows_of, NT).astype(jnp.bfloat16)
            for piece in range(PIECES):
                src_ref[way, l, f * PIECES + piece, c * half : (c + 1) * half, :] = picked[
                    piece * half : (piece + 1) * half
                ]

    fronts = [(l, way) for l in range(subs) for way in range(2)]

    def first(v, ch):
        for l, way in fronts:

            @pl.when(depth(l, way) == v)
            def _():
                send(src_ref.at[way, l, ch], l, way, v, ch)
                val[way, l, v, ch] = src_ref[way, l, ch]

    def begin(f, _):
        for l, way in fronts:

            @pl.when(depth(l, way) <= spare)
            def _():
                pick(way, l, f)

        @pl.when(f == 0)
        def _():
            pl.semaphore_wait(barrier, 5)

        for v in range(spare + 1):
            lax.fori_loop(
                f * PIECES, (f + 1) * PIECES, lambda ch, _: (first(v, ch), 0)[1], 0
            )
        return 0

    lax.fori_loop(0, freqs, begin, 0)
    for l, way in fronts:

        @pl.when(depth(l, way) > spare)
        def _():
            for f in range(freqs if spare else 1):
                pick(way, l, f)

    for f, l in every:
        map_load(0, f, l).wait()
    for f, l in every:
        map_load(1, f, l).start()

    def step(t, v, ch, l, way):
        f = ch // PIECES
        above, beside, _, _, far_in, _, near = edges(l, way)

        @pl.when(above)
        def _():
            copy_of(val.at[way, l, v, ch], way, 1 + l, v, ch, reach).wait_recv()
            hands = handed(l, way)
            if hands is not None:

                @pl.when(hands)
                def _():
                    hand_on(way, l, v, ch).start()

            xin[...] = recv[way, 1 + l, v, ch]

        @pl.when(jnp.logical_not(above))
        def _():
            xin[...] = jnp.zeros_like(xin)

        @pl.when(beside)
        def _():
            if far_in:
                copy_of(val.at[way, l, v, ch], way, 0, v, ch, 1).wait_recv()
                side = recv[way, 0, v, ch]
            else:
                side = val[way, near, v, ch]
            xin[...] = (xin[...].astype(jnp.float32) + side.astype(jnp.float32)).astype(
                jnp.bfloat16
            )

        x = xin[...]
        for n in range(0, width, COLS):
            span = slice(n, n + COLS)
            if way == 0:
                p = dot(x, trace[f, l, 0, span, :], NT)
                s = dot(x, trace[f, l, 1, span, :], NT)
                real, imag = p[:half] - s[half:], p[half:] + s[:half]
            else:
                p = dot(x, trace[f, l, 0, :, span], NN)
                s = dot(x, trace[f, l, 1, :, span], NN)
                real, imag = p[:half] + s[half:], p[half:] - s[:half]
            mine = src_ref[way, l, ch, :, span].astype(jnp.float32)
            val[way, l, v, ch, :half, span] = (mine[:half] + real).astype(jnp.bfloat16)
            val[way, l, v, ch, half:, span] = (mine[half:] + imag).astype(jnp.bfloat16)

        @pl.when(t < TICKS)
        def _():
            send(val.at[way, l, v, ch], l, way, v, ch)

        if spare == 0:

            @pl.when(both(lax.rem(ch, PIECES) == 1, f + 1 < freqs))
            def _():
                pick(way, l, f + 1)

    width_half = width // 2
    keep = pl.ds(pl.multiple_of(q * width_half, width_half), width_half)
    give = pl.ds(pl.multiple_of(other * width_half, width_half), width_half)

    def swaps(l, f):
        for k, (src, dst) in enumerate(
            (
                (wave.at[l, f, :, give], left_hbm.at[l, freqs + f]),
                (back.at[l, f], right_hbm.at[l, freqs + f]),
            )
        ):
            yield pltpu.make_async_remote_copy(
                src_ref=src,
                dst_ref=dst,
                send_sem=swap_send.at[k, l, f],
                recv_sem=swap_recv.at[k, l, f],
                device_id={"freq": other},
                device_id_type=MESH,
            )

    def keeps(l, f):
        for k, (src, dst) in enumerate(
            (
                (wave.at[l, f, :, keep], left_hbm.at[l, f]),
                (back.at[l, f], right_hbm.at[l, f]),
            )
        ):
            yield pltpu.make_async_copy(src, dst, keep_sem.at[k, l, f])

    def inside(l, f):
        map_load(1, f, l).wait()
        stack = []
        for way in range(2):
            v = 0 if spare == 0 else jnp.maximum(depth(l, way) - TICKS, 0)
            for piece in range(PIECES):
                stack.append(val[way, l, v, f * PIECES + piece])
        x = jnp.concatenate(stack, axis=0)
        high = x.shape[0] // 2
        for n in range(0, width, COLS):
            span = slice(n, n + COLS)
            p = dot(x, interior[f, l, 0, span, :], NT)
            s = dot(x, interior[f, l, 1, span, :], NT)
            p = p.reshape(-1, 2, half, COLS)
            s = s.reshape(-1, 2, half, COLS)
            y = jnp.stack([p[:, 0] - s[:, 1], p[:, 1] + s[:, 0]], axis=1)
            y = y.reshape(2, high, COLS).astype(jnp.bfloat16)
            wave[l, f, :, span] = y[0]
            back[l, f, :, span] = y[1]
        for copy in (*swaps(l, f), *keeps(l, f)):
            copy.start()

    kinds = []
    for l in range(subs):
        for way in range(2):
            r, c = place(l)
            for v in range(spare + 1):
                t = depth(l, way) - v
                begin, pace = 60 * t, 300
                if (count, total, spare) == (8, 16, 0):
                    for g in range(total):
                        here = r * GY + c == g
                        begin = jnp.where(here, FIRST[way][g], begin)
                        pace = jnp.where(here, EVERY[way][g], pace)
                kinds.append((l, way, v, t, both(t >= 1, t <= TICKS), begin * 10, pace))
    jobs = chunks * sum(valid.astype(jnp.int32) for *_, valid, _, _ in kinds)

    def corner(l):
        return jnp.logical_or(depth(l, 0) == 0, depth(l, 1) == 0)

    def turn(_, done):
        due = [
            jnp.where(both(valid, n < chunks), begin + pace * n, LATE)
            for n, (*_, valid, begin, pace) in zip(done, kinds)
        ]
        least = functools.reduce(jnp.minimum, due)
        free = jnp.bool_(True)
        after = []
        for n, time, (l, way, v, t, *_) in zip(done, due, kinds):
            mine = both(free, time == least)
            free = both(free, jnp.logical_not(mine))

            @pl.when(mine)
            def _():
                step(t, v, n, l, way)
                if spare == 0:

                    @pl.when(both(corner(l), lax.rem(n, PIECES) == PIECES - 1))
                    def _():
                        inside(l, n // PIECES)

            after.append(n + mine.astype(jnp.int32))
        return tuple(after)

    lax.fori_loop(0, jobs, turn, tuple(jnp.int32(0) for _ in kinds))

    for l in range(subs):

        @pl.when(jnp.logical_not(corner(l)) if spare == 0 else l >= 0)
        def _():
            lax.fori_loop(0, freqs, lambda f, _: (inside(l, f), 0)[1], 0)

    def finish(v, ch):
        for l in range(subs):
            for way in range(2):
                here = depth(l, way)
                _, _, below, aside, _, far_out, _ = edges(l, way)
                sent = jnp.logical_and(here >= v, here < v + TICKS)
                if far_out:

                    @pl.when(both(sent, direct(way, aside, below)))
                    def _():
                        copy_of(val.at[way, l, v, ch], way, 0, v, ch, 1).wait_send()

                hands = handed(l, way)
                if hands is not None:

                    @pl.when(both(hands, here - v >= 1, here - v <= TICKS))
                    def _():
                        hand_on(way, l, v, ch).wait_send()

                @pl.when(jnp.logical_and(sent, below))
                def _():
                    copy_of(val.at[way, l, v, ch], way, 1 + l, v, ch, reach).wait_send()

    each(finish)
    for f, l in every:
        for copy in (*swaps(l, f), *keeps(l, f)):
            copy.wait()


def per_device(trace_map, interior_map, excitation, receiver_data, shot_index):
    freqs, subs, _, width, _ = trace_map.shape
    shots = shot_index.shape[0]
    bank = excitation.shape[4]
    count = lax.axis_size("sub")
    half = shots // PIECES
    chunks = freqs * PIECES
    rows = count * subs // GY
    spare = max(0, rows + GY - 2 - TICKS)
    scale = (2.0 * shots * freqs * lax.axis_size("freq")) ** (-0.5)
    bf = jnp.bfloat16
    flat = (freqs, subs, 2 * width, bank)
    dma = pltpu.SemaphoreType.DMA
    front = (chunks, 2 * half, width)
    left, right = pl.pallas_call(
        functools.partial(sweep, count, freqs, subs),
        out_shape=[
            jax.ShapeDtypeStruct((subs, 2 * freqs, 2 * shots, width // 2), bf),
            jax.ShapeDtypeStruct((subs, 2 * freqs, 2 * shots, width), bf),
        ],
        in_specs=[pl.BlockSpec(memory_space=pltpu.HBM)] * 4
        + [pl.BlockSpec(memory_space=pltpu.VMEM)],
        out_specs=[pl.BlockSpec(memory_space=pl.ANY)] * 2,
        scratch_shapes=[
            pltpu.VMEM(trace_map.shape, bf),
            pltpu.VMEM(interior_map.shape, bf),
            pltpu.VMEM((2, subs, freqs, 2 * width, bank), bf),
            pltpu.VMEM((2 * width, bank), jnp.float32),
            pltpu.VMEM((2, subs) + front, bf),
            pltpu.VMEM((2, subs, spare + 1) + front, bf),
            pltpu.VMEM((2, subs + 1, spare + 1) + front, bf),
            pltpu.VMEM((2 * half, width), bf),
            pltpu.VMEM((subs, freqs, 2 * shots, width), bf),
            pltpu.VMEM((subs, freqs, 2 * shots, width), bf),
            dma((2, freqs, subs)),
            dma((2, subs, freqs)),
            dma((2, subs + 1, spare + 1, chunks)),
            dma((2, subs + 1, spare + 1, chunks)),
            dma((2, spare + 1, chunks)),
            dma((2, subs, freqs)),
            dma((2, subs, freqs)),
            dma((2, subs, freqs)),
        ],
        compiler_params=pltpu.CompilerParams(
            collective_id=0, has_side_effects=True, vmem_limit_bytes=VMEM
        ),
    )(
        trace_map,
        interior_map,
        excitation.reshape(flat),
        receiver_data.reshape(flat),
        shot_index.reshape(1, shots),
    )
    image = jnp.einsum("sfma,sfmc->sac", left, right, preferred_element_type=jnp.float32)
    return image * scale


def solution(mesh):
    placed = (
        P("freq", ("survey", "sub"), None, None, None),
        P("freq", ("survey", "sub"), None, None, None),
        P("freq", ("survey", "sub"), None, None, None),
        P("freq", ("survey", "sub"), None, None, None),
        P("survey"),
    )
    return jax.shard_map(
        per_device,
        mesh=mesh,
        in_specs=placed,
        out_specs=P(("survey", "sub"), "freq", None),
        check_vma=False,
    )
```

```python
import functools

import jax
import jax.numpy as jnp
from jax import lax
from jax.experimental import pallas as pl
from jax.experimental.pallas import tpu as pltpu
from jax.sharding import PartitionSpec as P

GY = 4
TICKS = 6
PIECES = 4
VMEM = 51 << 20
LATE = 1 << 20
FIRST = (
    (0, 61, 75, 163, 15, 143, 179, 368, 150, 231, 240, 212, 128, 288, 293, 384),
    (478, 309, 112, 148, 589, 141, 132, 119, 409, 96, 79, 5, 98, 44, 42, 0),
)
EVERY = (
    (0, 234, 226, 74, 107, 436, 418, 186, 144, 337, 359, 412, 30, 535, 528, 654),
    (428, 206, 470, 156, 340, 438, 406, 272, 104, 382, 355, 194, 363, 103, 105, 0),
)
COLS = 256
MESH = pl.DeviceIdType.MESH
NT = (((1,), (1,)), ((), ()))
NN = (((1,), (0,)), ((), ()))


def dot(a, b, dims):
    return lax.dot_general(a, b, dims, preferred_element_type=jnp.float32)


def sweep(
    count,
    freqs,
    subs,
    trace_hbm,
    interior_hbm,
    fired_hbm,
    heard_hbm,
    shot_ref,
    left_hbm,
    right_hbm,
    trace,
    interior,
    bank,
    plain,
    src_ref,
    val,
    recv,
    xin,
    wave,
    back,
    load_sem,
    bank_sem,
    send_sem,
    recv_sem,
    hand_sem,
    swap_send,
    swap_recv,
    keep_sem,
):
    total = count * subs
    rows = total // GY
    deepest = rows - 1 + GY - 1
    spare = max(0, deepest - TICKS)
    reach = GY // subs
    chunks = freqs * PIECES
    width = val.shape[-1]
    tall = val.shape[-2]
    half = tall // 2
    me = lax.axis_index("sub")
    q = lax.axis_index("freq")
    other = 1 - q

    def bank_load(way, l, f):
        hbm = (fired_hbm, heard_hbm)[way]
        return pltpu.make_async_copy(hbm.at[f, l], bank.at[way, l, f], bank_sem.at[way, l, f])

    def map_load(m, f, l):
        hbm, vmem = ((trace_hbm, trace), (interior_hbm, interior))[m]
        return pltpu.make_async_copy(hbm.at[f, l], vmem.at[f, l], load_sem.at[m, f, l])

    every = [(f, l) for f in range(freqs) for l in range(subs)]
    for f, l in every:
        for way in range(2):
            bank_load(way, l, f).start()
    for f, l in every:
        map_load(0, f, l).start()

    barrier = pltpu.get_barrier_semaphore()
    for by in (1, count - 1, reach, count - reach):
        pl.semaphore_signal(
            barrier, inc=1, device_id={"sub": lax.rem(me + by, count)}, device_id_type=MESH
        )
    pl.semaphore_signal(barrier, inc=1, device_id={"freq": other}, device_id_type=MESH)

    def place(l):
        g = lax.rem(me * subs + l + GY + 1, total)
        return g // GY, lax.rem(g, GY)

    def depth(l, way):
        r, c = place(l)
        return r + c if way == 0 else deepest - r - c

    def copy_of(ref, way, slot, v, ch, by, sem=None):
        return pltpu.make_async_remote_copy(
            src_ref=ref,
            dst_ref=recv.at[way, slot, v, ch],
            send_sem=send_sem.at[way, slot, v, ch] if sem is None else sem,
            recv_sem=recv_sem.at[way, slot, v, ch],
            device_id={"sub": lax.rem(me + (by if way == 0 else count - by), count)},
            device_id_type=MESH,
        )

    def edges(l, way):
        r, c = place(l)
        if way == 0:
            return r > 0, c > 0, r < rows - 1, c < GY - 1, l == 0, l == subs - 1, l - 1
        return r < rows - 1, c < GY - 1, r > 0, c > 0, l == subs - 1, l == 0, l + 1

    relays = reach == 2 and count % 2 == 0
    parity = lax.rem(me, 2)

    def both(*flags):
        return functools.reduce(jnp.logical_and, flags)

    def send(ref, l, way, v, ch):
        _, _, below, aside, _, far_out, _ = edges(l, way)

        @pl.when(below)
        def _():
            copy_of(ref, way, 1 + l, v, ch, reach).start()

        if far_out:

            @pl.when(direct(way, aside, below))
            def _():
                copy_of(ref, way, 0, v, ch, 1).start()

    def direct(way, aside, below):
        if not relays:
            return aside
        return both(aside, jnp.logical_not(both(parity == 1 - way, below)))

    def handed(l, way):
        above, _, _, _, _, far_out, _ = edges(l, way)
        return both(parity == 1 - way, above) if relays and far_out else None

    def hand_on(way, l, v, ch):
        return copy_of(
            recv.at[way, 1 + l, v, ch], way, 0, v, ch, count - 1, sem=hand_sem.at[way, v, ch]
        )

    def each(body):
        if spare == 0:
            lax.fori_loop(0, chunks, lambda ch, _: (body(0, ch), 0)[1], 0)
        else:

            def outer(v, _):
                lax.fori_loop(0, chunks, lambda ch, _: (body(v, ch), 0)[1], 0)
                return 0

            lax.fori_loop(0, spare + 1, outer, 0)

    shots = shot_ref.shape[1]
    number = lax.broadcasted_iota(jnp.int32, (bank.shape[-1], shots), 0)
    chooser = jnp.transpose((number == shot_ref[...]).astype(jnp.float32)).astype(jnp.bfloat16)

    def pick(way, l, f):
        bank_load(way, l, f).wait()
        plain[...] = bank[way, l, f].astype(jnp.float32)
        for c in range(2):
            rows_of = plain[pl.ds(c, width, stride=2), :].astype(jnp.bfloat16)
            picked = dot(chooser, rows_of, NT).astype(jnp.bfloat16)
            for piece in range(PIECES):
                src_ref[way, l, f * PIECES + piece, c * half : (c + 1) * half, :] = picked[
                    piece * half : (piece + 1) * half
                ]

    fronts = [(l, way) for l in range(subs) for way in range(2)]

    def first(v, ch):
        for l, way in fronts:

            @pl.when(depth(l, way) == v)
            def _():
                send(src_ref.at[way, l, ch], l, way, v, ch)
                val[way, l, v, ch] = src_ref[way, l, ch]

    def begin(f, _):
        for l, way in fronts:

            @pl.when(depth(l, way) <= spare)
            def _():
                pick(way, l, f)

        @pl.when(f == 0)
        def _():
            pl.semaphore_wait(barrier, 5)

        for v in range(spare + 1):
            lax.fori_loop(
                f * PIECES, (f + 1) * PIECES, lambda ch, _: (first(v, ch), 0)[1], 0
            )
        return 0

    lax.fori_loop(0, freqs, begin, 0)
    for l, way in fronts:

        @pl.when(depth(l, way) > spare)
        def _():
            for f in range(freqs if spare else 1):
                pick(way, l, f)

    for f, l in every:
        map_load(0, f, l).wait()
    for f, l in every:
        map_load(1, f, l).start()

    def step(t, v, ch, l, way):
        f = ch // PIECES
        above, beside, _, _, far_in, _, near = edges(l, way)

        @pl.when(above)
        def _():
            copy_of(val.at[way, l, v, ch], way, 1 + l, v, ch, reach).wait_recv()
            hands = handed(l, way)
            if hands is not None:

                @pl.when(hands)
                def _():
                    hand_on(way, l, v, ch).start()

            xin[...] = recv[way, 1 + l, v, ch]

        @pl.when(jnp.logical_not(above))
        def _():
            xin[...] = jnp.zeros_like(xin)

        @pl.when(beside)
        def _():
            if far_in:
                copy_of(val.at[way, l, v, ch], way, 0, v, ch, 1).wait_recv()
                side = recv[way, 0, v, ch]
            else:
                side = val[way, near, v, ch]
            xin[...] = (xin[...].astype(jnp.float32) + side.astype(jnp.float32)).astype(
                jnp.bfloat16
            )

        x = xin[...]
        for n in range(0, width, COLS):
            span = slice(n, n + COLS)
            if way == 0:
                p = dot(x, trace[f, l, 0, span, :], NT)
                s = dot(x, trace[f, l, 1, span, :], NT)
                real, imag = p[:half] - s[half:], p[half:] + s[:half]
            else:
                p = dot(x, trace[f, l, 0, :, span], NN)
                s = dot(x, trace[f, l, 1, :, span], NN)
                real, imag = p[:half] + s[half:], p[half:] - s[:half]
            mine = src_ref[way, l, ch, :, span].astype(jnp.float32)
            val[way, l, v, ch, :half, span] = (mine[:half] + real).astype(jnp.bfloat16)
            val[way, l, v, ch, half:, span] = (mine[half:] + imag).astype(jnp.bfloat16)

        @pl.when(t < TICKS)
        def _():
            send(val.at[way, l, v, ch], l, way, v, ch)

        if spare == 0:

            @pl.when(both(lax.rem(ch, PIECES) == 1, f + 1 < freqs))
            def _():
                pick(way, l, f + 1)

    width_half = width // 2
    keep = pl.ds(pl.multiple_of(q * width_half, width_half), width_half)
    give = pl.ds(pl.multiple_of(other * width_half, width_half), width_half)

    def swaps(l, f):
        for k, (src, dst) in enumerate(
            (
                (wave.at[l, f, :, give], left_hbm.at[l, freqs + f]),
                (back.at[l, f], right_hbm.at[l, freqs + f]),
            )
        ):
            yield pltpu.make_async_remote_copy(
                src_ref=src,
                dst_ref=dst,
                send_sem=swap_send.at[k, l, f],
                recv_sem=swap_recv.at[k, l, f],
                device_id={"freq": other},
                device_id_type=MESH,
            )

    def keeps(l, f):
        for k, (src, dst) in enumerate(
            (
                (wave.at[l, f, :, keep], left_hbm.at[l, f]),
                (back.at[l, f], right_hbm.at[l, f]),
            )
        ):
            yield pltpu.make_async_copy(src, dst, keep_sem.at[k, l, f])

    def inside(l, f):
        map_load(1, f, l).wait()
        stack = []
        for way in range(2):
            v = 0 if spare == 0 else jnp.maximum(depth(l, way) - TICKS, 0)
            for piece in range(PIECES):
                stack.append(val[way, l, v, f * PIECES + piece])
        x = jnp.concatenate(stack, axis=0)
        high = x.shape[0] // 2
        for n in range(0, width, COLS):
            span = slice(n, n + COLS)
            p = dot(x, interior[f, l, 0, span, :], NT)
            s = dot(x, interior[f, l, 1, span, :], NT)
            p = p.reshape(-1, 2, half, COLS)
            s = s.reshape(-1, 2, half, COLS)
            y = jnp.stack([p[:, 0] - s[:, 1], p[:, 1] + s[:, 0]], axis=1)
            y = y.reshape(2, high, COLS).astype(jnp.bfloat16)
            wave[l, f, :, span] = y[0]
            back[l, f, :, span] = y[1]
        for copy in (*swaps(l, f), *keeps(l, f)):
            copy.start()

    kinds = []
    for l in range(subs):
        for way in range(2):
            r, c = place(l)
            for v in range(spare + 1):
                t = depth(l, way) - v
                begin, pace = 60 * t, 300
                if (count, total, spare) == (8, 16, 0):
                    for g in range(total):
                        here = r * GY + c == g
                        begin = jnp.where(here, FIRST[way][g], begin)
                        pace = jnp.where(here, EVERY[way][g], pace)
                kinds.append((l, way, v, t, both(t >= 1, t <= TICKS), begin * 10, pace))
    jobs = chunks * sum(valid.astype(jnp.int32) for *_, valid, _, _ in kinds)

    def corner(l):
        return jnp.logical_or(depth(l, 0) == 0, depth(l, 1) == 0)

    def turn(_, done):
        due = [
            jnp.where(both(valid, n < chunks), begin + pace * n, LATE)
            for n, (*_, valid, begin, pace) in zip(done, kinds)
        ]
        least = functools.reduce(jnp.minimum, due)
        free = jnp.bool_(True)
        after = []
        for n, time, (l, way, v, t, *_) in zip(done, due, kinds):
            mine = both(free, time == least)
            free = both(free, jnp.logical_not(mine))

            @pl.when(mine)
            def _():
                step(t, v, n, l, way)
                if spare == 0:

                    @pl.when(both(corner(l), lax.rem(n, PIECES) == PIECES - 1))
                    def _():
                        inside(l, n // PIECES)

            after.append(n + mine.astype(jnp.int32))
        return tuple(after)

    lax.fori_loop(0, jobs, turn, tuple(jnp.int32(0) for _ in kinds))

    for l in range(subs):

        @pl.when(jnp.logical_not(corner(l)) if spare == 0 else l >= 0)
        def _():
            lax.fori_loop(0, freqs, lambda f, _: (inside(l, f), 0)[1], 0)

    def finish(v, ch):
        for l in range(subs):
            for way in range(2):
                here = depth(l, way)
                _, _, below, aside, _, far_out, _ = edges(l, way)
                sent = jnp.logical_and(here >= v, here < v + TICKS)
                if far_out:

                    @pl.when(both(sent, direct(way, aside, below)))
                    def _():
                        copy_of(val.at[way, l, v, ch], way, 0, v, ch, 1).wait_send()

                hands = handed(l, way)
                if hands is not None:

                    @pl.when(both(hands, here - v >= 1, here - v <= TICKS))
                    def _():
                        hand_on(way, l, v, ch).wait_send()

                @pl.when(jnp.logical_and(sent, below))
                def _():
                    copy_of(val.at[way, l, v, ch], way, 1 + l, v, ch, reach).wait_send()

    each(finish)
    for f, l in every:
        for copy in (*swaps(l, f), *keeps(l, f)):
            copy.wait()


def per_device(trace_map, interior_map, excitation, receiver_data, shot_index):
    freqs, subs, _, width, _ = trace_map.shape
    shots = shot_index.shape[0]
    bank = excitation.shape[4]
    count = lax.axis_size("sub")
    half = shots // PIECES
    chunks = freqs * PIECES
    rows = count * subs // GY
    spare = max(0, rows + GY - 2 - TICKS)
    scale = (2.0 * shots * freqs * lax.axis_size("freq")) ** (-0.5)
    bf = jnp.bfloat16
    flat = (freqs, subs, 2 * width, bank)
    dma = pltpu.SemaphoreType.DMA
    front = (chunks, 2 * half, width)
    left, right = pl.pallas_call(
        functools.partial(sweep, count, freqs, subs),
        out_shape=[
            jax.ShapeDtypeStruct((subs, 2 * freqs, 2 * shots, width // 2), bf),
            jax.ShapeDtypeStruct((subs, 2 * freqs, 2 * shots, width), bf),
        ],
        in_specs=[pl.BlockSpec(memory_space=pltpu.HBM)] * 4
        + [pl.BlockSpec(memory_space=pltpu.VMEM)],
        out_specs=[pl.BlockSpec(memory_space=pl.ANY)] * 2,
        scratch_shapes=[
            pltpu.VMEM(trace_map.shape, bf),
            pltpu.VMEM(interior_map.shape, bf),
            pltpu.VMEM((2, subs, freqs, 2 * width, bank), bf),
            pltpu.VMEM((2 * width, bank), jnp.float32),
            pltpu.VMEM((2, subs) + front, bf),
            pltpu.VMEM((2, subs, spare + 1) + front, bf),
            pltpu.VMEM((2, subs + 1, spare + 1) + front, bf),
            pltpu.VMEM((2 * half, width), bf),
            pltpu.VMEM((subs, freqs, 2 * shots, width), bf),
            pltpu.VMEM((subs, freqs, 2 * shots, width), bf),
            dma((2, freqs, subs)),
            dma((2, subs, freqs)),
            dma((2, subs + 1, spare + 1, chunks)),
            dma((2, subs + 1, spare + 1, chunks)),
            dma((2, spare + 1, chunks)),
            dma((2, subs, freqs)),
            dma((2, subs, freqs)),
            dma((2, subs, freqs)),
        ],
        compiler_params=pltpu.CompilerParams(
            collective_id=0, has_side_effects=True, vmem_limit_bytes=VMEM
        ),
    )(
        trace_map,
        interior_map,
        excitation.reshape(flat),
        receiver_data.reshape(flat),
        shot_index.reshape(1, shots),
    )
    image = jnp.einsum("sfma,sfmc->sac", left, right, preferred_element_type=jnp.float32)
    return image * scale


def solution(mesh):
    placed = (
        P("freq", ("survey", "sub"), None, None, None),
        P("freq", ("survey", "sub"), None, None, None),
        P("freq", ("survey", "sub"), None, None, None),
        P("freq", ("survey", "sub"), None, None, None),
        P("survey"),
    )
    return jax.shard_map(
        per_device,
        mesh=mesh,
        in_specs=placed,
        out_specs=P(("survey", "sub"), "freq", None),
        check_vma=False,
    )
```

```python
import functools

import jax
import jax.numpy as jnp
from jax import lax
from jax.experimental import pallas as pl
from jax.experimental.pallas import tpu as pltpu
from jax.sharding import PartitionSpec as P

GY = 4
TICKS = 6
PIECES = 4
VMEM = 51 << 20
LATE = 1 << 20
FIRST = (
    (0, 61, 75, 201, 15, 143, 172, 368, 150, 221, 240, 212, 130, 288, 293, 377),
    (514, 309, 112, 148, 589, 141, 112, 119, 421, 85, 79, 5, 98, 44, 29, 0),
)
EVERY = (
    (0, 234, 218, 74, 107, 436, 428, 186, 137, 335, 359, 412, 30, 535, 528, 664),
    (386, 206, 470, 156, 275, 438, 434, 272, 88, 382, 384, 183, 363, 103, 123, 0),
)
COLS = 256
MESH = pl.DeviceIdType.MESH
NT = (((1,), (1,)), ((), ()))
NN = (((1,), (0,)), ((), ()))


def dot(a, b, dims):
    return lax.dot_general(a, b, dims, preferred_element_type=jnp.float32)


def sweep(
    count,
    freqs,
    subs,
    trace_hbm,
    interior_hbm,
    fired_hbm,
    heard_hbm,
    shot_ref,
    left_hbm,
    right_hbm,
    trace,
    interior,
    bank,
    plain,
    src_ref,
    val,
    recv,
    xin,
    wave,
    back,
    load_sem,
    bank_sem,
    send_sem,
    recv_sem,
    hand_sem,
    swap_send,
    swap_recv,
    keep_sem,
):
    total = count * subs
    rows = total // GY
    deepest = rows - 1 + GY - 1
    spare = max(0, deepest - TICKS)
    reach = GY // subs
    chunks = freqs * PIECES
    width = val.shape[-1]
    tall = val.shape[-2]
    half = tall // 2
    me = lax.axis_index("sub")
    q = lax.axis_index("freq")
    other = 1 - q

    def place(l):
        g = lax.rem(me * subs + l + GY + 1, total)
        return g // GY, lax.rem(g, GY)

    def depth(l, way):
        r, c = place(l)
        return r + c if way == 0 else deepest - r - c

    def bank_load(way, l, f):
        hbm = (fired_hbm, heard_hbm)[way]
        return pltpu.make_async_copy(hbm.at[f, l], bank.at[way, l, f], bank_sem.at[way, l, f])

    def map_load(m, f, l):
        hbm, vmem = ((trace_hbm, trace), (interior_hbm, interior))[m]
        return pltpu.make_async_copy(hbm.at[f, l], vmem.at[f, l], load_sem.at[m, f, l])

    every = [(f, l) for f in range(freqs) for l in range(subs)]
    fronts = [(l, way) for l in range(subs) for way in range(2)]

    def early(l, way):
        return depth(l, way) <= spare

    source = functools.reduce(jnp.logical_or, [early(l, way) for l, way in fronts])

    def load_rest():
        for f in range(freqs):
            for l, way in fronts:

                @pl.when(jnp.logical_not(early(l, way)))
                def _():
                    bank_load(way, l, f).start()

        for f, l in every:
            map_load(0, f, l).start()

    for f in range(freqs):
        for l, way in fronts:

            @pl.when(early(l, way))
            def _():
                bank_load(way, l, f).start()

    @pl.when(jnp.logical_not(source))
    def _():
        load_rest()

    barrier = pltpu.get_barrier_semaphore()
    for by in (1, count - 1, reach, count - reach):
        pl.semaphore_signal(
            barrier, inc=1, device_id={"sub": lax.rem(me + by, count)}, device_id_type=MESH
        )
    pl.semaphore_signal(barrier, inc=1, device_id={"freq": other}, device_id_type=MESH)

    def copy_of(ref, way, slot, v, ch, by, sem=None):
        return pltpu.make_async_remote_copy(
            src_ref=ref,
            dst_ref=recv.at[way, slot, v, ch],
            send_sem=send_sem.at[way, slot, v, ch] if sem is None else sem,
            recv_sem=recv_sem.at[way, slot, v, ch],
            device_id={"sub": lax.rem(me + (by if way == 0 else count - by), count)},
            device_id_type=MESH,
        )

    def edges(l, way):
        r, c = place(l)
        if way == 0:
            return r > 0, c > 0, r < rows - 1, c < GY - 1, l == 0, l == subs - 1, l - 1
        return r < rows - 1, c < GY - 1, r > 0, c > 0, l == subs - 1, l == 0, l + 1

    relays = reach == 2 and count % 2 == 0
    parity = lax.rem(me, 2)

    def both(*flags):
        return functools.reduce(jnp.logical_and, flags)

    def send(ref, l, way, v, ch):
        _, _, below, aside, _, far_out, _ = edges(l, way)

        @pl.when(below)
        def _():
            copy_of(ref, way, 1 + l, v, ch, reach).start()

        if far_out:

            @pl.when(direct(way, aside, below))
            def _():
                copy_of(ref, way, 0, v, ch, 1).start()

    def direct(way, aside, below):
        if not relays:
            return aside
        return both(aside, jnp.logical_not(both(parity == 1 - way, below)))

    def handed(l, way):
        above, _, _, _, _, far_out, _ = edges(l, way)
        return both(parity == 1 - way, above) if relays and far_out else None

    def hand_on(way, l, v, ch):
        return copy_of(
            recv.at[way, 1 + l, v, ch], way, 0, v, ch, count - 1, sem=hand_sem.at[way, v, ch]
        )

    def each(body):
        if spare == 0:
            lax.fori_loop(0, chunks, lambda ch, _: (body(0, ch), 0)[1], 0)
        else:

            def outer(v, _):
                lax.fori_loop(0, chunks, lambda ch, _: (body(v, ch), 0)[1], 0)
                return 0

            lax.fori_loop(0, spare + 1, outer, 0)

    shots = shot_ref.shape[1]
    number = lax.broadcasted_iota(jnp.int32, (bank.shape[-1], shots), 0)
    chooser = jnp.transpose((number == shot_ref[...]).astype(jnp.float32)).astype(jnp.bfloat16)

    def pick(way, l, f):
        bank_load(way, l, f).wait()
        plain[...] = bank[way, l, f].astype(jnp.float32)
        for c in range(2):
            rows_of = plain[pl.ds(c, width, stride=2), :].astype(jnp.bfloat16)
            picked = dot(chooser, rows_of, NT).astype(jnp.bfloat16)
            for piece in range(PIECES):
                src_ref[way, l, f * PIECES + piece, c * half : (c + 1) * half, :] = picked[
                    piece * half : (piece + 1) * half
                ]

    def first(v, ch):
        for l, way in fronts:

            @pl.when(depth(l, way) == v)
            def _():
                send(src_ref.at[way, l, ch], l, way, v, ch)
                val[way, l, v, ch] = src_ref[way, l, ch]

    def begin(f, _):
        for l, way in fronts:

            @pl.when(early(l, way))
            def _():
                pick(way, l, f)

        @pl.when(f == 0)
        def _():
            pl.semaphore_wait(barrier, 5)

        for v in range(spare + 1):
            lax.fori_loop(
                f * PIECES, (f + 1) * PIECES, lambda ch, _: (first(v, ch), 0)[1], 0
            )
        return 0

    lax.fori_loop(0, freqs, begin, 0)

    @pl.when(source)
    def _():
        load_rest()

    for l, way in fronts:

        @pl.when(jnp.logical_not(early(l, way)))
        def _():
            for f in range(freqs if spare else 1):
                pick(way, l, f)

    for f, l in every:
        map_load(0, f, l).wait()
    for f, l in every:
        map_load(1, f, l).start()

    def step(t, v, ch, l, way):
        f = ch // PIECES
        above, beside, _, _, far_in, _, near = edges(l, way)

        @pl.when(above)
        def _():
            copy_of(val.at[way, l, v, ch], way, 1 + l, v, ch, reach).wait_recv()
            hands = handed(l, way)
            if hands is not None:

                @pl.when(hands)
                def _():
                    hand_on(way, l, v, ch).start()

            xin[...] = recv[way, 1 + l, v, ch]

        @pl.when(jnp.logical_not(above))
        def _():
            xin[...] = jnp.zeros_like(xin)

        @pl.when(beside)
        def _():
            if far_in:
                copy_of(val.at[way, l, v, ch], way, 0, v, ch, 1).wait_recv()
                side = recv[way, 0, v, ch]
            else:
                side = val[way, near, v, ch]
            xin[...] = (xin[...].astype(jnp.float32) + side.astype(jnp.float32)).astype(
                jnp.bfloat16
            )

        x = xin[...]
        for n in range(0, width, COLS):
            span = slice(n, n + COLS)
            if way == 0:
                p = dot(x, trace[f, l, 0, span, :], NT)
                s = dot(x, trace[f, l, 1, span, :], NT)
                real, imag = p[:half] - s[half:], p[half:] + s[:half]
            else:
                p = dot(x, trace[f, l, 0, :, span], NN)
                s = dot(x, trace[f, l, 1, :, span], NN)
                real, imag = p[:half] + s[half:], p[half:] - s[:half]
            mine = src_ref[way, l, ch, :, span].astype(jnp.float32)
            val[way, l, v, ch, :half, span] = (mine[:half] + real).astype(jnp.bfloat16)
            val[way, l, v, ch, half:, span] = (mine[half:] + imag).astype(jnp.bfloat16)

        @pl.when(t < TICKS)
        def _():
            send(val.at[way, l, v, ch], l, way, v, ch)

        if spare == 0:

            @pl.when(both(lax.rem(ch, PIECES) == 1, f + 1 < freqs))
            def _():
                pick(way, l, f + 1)

    width_half = width // 2
    keep = pl.ds(pl.multiple_of(q * width_half, width_half), width_half)
    give = pl.ds(pl.multiple_of(other * width_half, width_half), width_half)

    def swaps(l, f):
        for k, (src, dst) in enumerate(
            (
                (wave.at[l, f, :, give], left_hbm.at[l, freqs + f]),
                (back.at[l, f], right_hbm.at[l, freqs + f]),
            )
        ):
            yield pltpu.make_async_remote_copy(
                src_ref=src,
                dst_ref=dst,
                send_sem=swap_send.at[k, l, f],
                recv_sem=swap_recv.at[k, l, f],
                device_id={"freq": other},
                device_id_type=MESH,
            )

    def keeps(l, f):
        for k, (src, dst) in enumerate(
            (
                (wave.at[l, f, :, keep], left_hbm.at[l, f]),
                (back.at[l, f], right_hbm.at[l, f]),
            )
        ):
            yield pltpu.make_async_copy(src, dst, keep_sem.at[k, l, f])

    def inside(l, f):
        map_load(1, f, l).wait()
        stack = []
        for way in range(2):
            v = 0 if spare == 0 else jnp.maximum(depth(l, way) - TICKS, 0)
            for piece in range(PIECES):
                stack.append(val[way, l, v, f * PIECES + piece])
        x = jnp.concatenate(stack, axis=0)
        high = x.shape[0] // 2
        for n in range(0, width, COLS):
            span = slice(n, n + COLS)
            p = dot(x, interior[f, l, 0, span, :], NT)
            s = dot(x, interior[f, l, 1, span, :], NT)
            p = p.reshape(-1, 2, half, COLS)
            s = s.reshape(-1, 2, half, COLS)
            y = jnp.stack([p[:, 0] - s[:, 1], p[:, 1] + s[:, 0]], axis=1)
            y = y.reshape(2, high, COLS).astype(jnp.bfloat16)
            wave[l, f, :, span] = y[0]
            back[l, f, :, span] = y[1]
        for copy in (*swaps(l, f), *keeps(l, f)):
            copy.start()

    kinds = []
    for l in range(subs):
        for way in range(2):
            r, c = place(l)
            for v in range(spare + 1):
                t = depth(l, way) - v
                begin, pace = 60 * t, 300
                if (count, total, spare) == (8, 16, 0):
                    for g in range(total):
                        here = r * GY + c == g
                        begin = jnp.where(here, FIRST[way][g], begin)
                        pace = jnp.where(here, EVERY[way][g], pace)
                kinds.append((l, way, v, t, both(t >= 1, t <= TICKS), begin * 10, pace))
    jobs = chunks * sum(valid.astype(jnp.int32) for *_, valid, _, _ in kinds)

    def corner(l):
        return jnp.logical_or(depth(l, 0) == 0, depth(l, 1) == 0)

    def turn(_, done):
        due = [
            jnp.where(both(valid, n < chunks), begin + pace * n, LATE)
            for n, (*_, valid, begin, pace) in zip(done, kinds)
        ]
        least = functools.reduce(jnp.minimum, due)
        free = jnp.bool_(True)
        after = []
        for n, time, (l, way, v, t, *_) in zip(done, due, kinds):
            mine = both(free, time == least)
            free = both(free, jnp.logical_not(mine))

            @pl.when(mine)
            def _():
                step(t, v, n, l, way)
                if spare == 0:

                    @pl.when(both(corner(l), lax.rem(n, PIECES) == PIECES - 1))
                    def _():
                        inside(l, n // PIECES)

            after.append(n + mine.astype(jnp.int32))
        return tuple(after)

    lax.fori_loop(0, jobs, turn, tuple(jnp.int32(0) for _ in kinds))

    for l in range(subs):

        @pl.when(jnp.logical_not(corner(l)) if spare == 0 else l >= 0)
        def _():
            lax.fori_loop(0, freqs, lambda f, _: (inside(l, f), 0)[1], 0)

    def finish(v, ch):
        for l in range(subs):
            for way in range(2):
                here = depth(l, way)
                _, _, below, aside, _, far_out, _ = edges(l, way)
                sent = jnp.logical_and(here >= v, here < v + TICKS)
                if far_out:

                    @pl.when(both(sent, direct(way, aside, below)))
                    def _():
                        copy_of(val.at[way, l, v, ch], way, 0, v, ch, 1).wait_send()

                hands = handed(l, way)
                if hands is not None:

                    @pl.when(both(hands, here - v >= 1, here - v <= TICKS))
                    def _():
                        hand_on(way, l, v, ch).wait_send()

                @pl.when(jnp.logical_and(sent, below))
                def _():
                    copy_of(val.at[way, l, v, ch], way, 1 + l, v, ch, reach).wait_send()

    each(finish)
    for f, l in every:
        for copy in (*swaps(l, f), *keeps(l, f)):
            copy.wait()


def per_device(trace_map, interior_map, excitation, receiver_data, shot_index):
    freqs, subs, _, width, _ = trace_map.shape
    shots = shot_index.shape[0]
    bank = excitation.shape[4]
    count = lax.axis_size("sub")
    half = shots // PIECES
    chunks = freqs * PIECES
    rows = count * subs // GY
    spare = max(0, rows + GY - 2 - TICKS)
    scale = (2.0 * shots * freqs * lax.axis_size("freq")) ** (-0.5)
    bf = jnp.bfloat16
    flat = (freqs, subs, 2 * width, bank)
    dma = pltpu.SemaphoreType.DMA
    front = (chunks, 2 * half, width)
    left, right = pl.pallas_call(
        functools.partial(sweep, count, freqs, subs),
        out_shape=[
            jax.ShapeDtypeStruct((subs, 2 * freqs, 2 * shots, width // 2), bf),
            jax.ShapeDtypeStruct((subs, 2 * freqs, 2 * shots, width), bf),
        ],
        in_specs=[pl.BlockSpec(memory_space=pltpu.HBM)] * 4
        + [pl.BlockSpec(memory_space=pltpu.VMEM)],
        out_specs=[pl.BlockSpec(memory_space=pl.ANY)] * 2,
        scratch_shapes=[
            pltpu.VMEM(trace_map.shape, bf),
            pltpu.VMEM(interior_map.shape, bf),
            pltpu.VMEM((2, subs, freqs, 2 * width, bank), bf),
            pltpu.VMEM((2 * width, bank), jnp.float32),
            pltpu.VMEM((2, subs) + front, bf),
            pltpu.VMEM((2, subs, spare + 1) + front, bf),
            pltpu.VMEM((2, subs + 1, spare + 1) + front, bf),
            pltpu.VMEM((2 * half, width), bf),
            pltpu.VMEM((subs, freqs, 2 * shots, width), bf),
            pltpu.VMEM((subs, freqs, 2 * shots, width), bf),
            dma((2, freqs, subs)),
            dma((2, subs, freqs)),
            dma((2, subs + 1, spare + 1, chunks)),
            dma((2, subs + 1, spare + 1, chunks)),
            dma((2, spare + 1, chunks)),
            dma((2, subs, freqs)),
            dma((2, subs, freqs)),
            dma((2, subs, freqs)),
        ],
        compiler_params=pltpu.CompilerParams(
            collective_id=0, has_side_effects=True, vmem_limit_bytes=VMEM
        ),
    )(
        trace_map,
        interior_map,
        excitation.reshape(flat),
        receiver_data.reshape(flat),
        shot_index.reshape(1, shots),
    )
    image = jnp.einsum("sfma,sfmc->sac", left, right, preferred_element_type=jnp.float32)
    return image * scale


def solution(mesh):
    placed = (
        P("freq", ("survey", "sub"), None, None, None),
        P("freq", ("survey", "sub"), None, None, None),
        P("freq", ("survey", "sub"), None, None, None),
        P("freq", ("survey", "sub"), None, None, None),
        P("survey"),
    )
    return jax.shard_map(
        per_device,
        mesh=mesh,
        in_specs=placed,
        out_specs=P(("survey", "sub"), "freq", None),
        check_vma=False,
    )
```

```python
import functools

import jax
import jax.numpy as jnp
from jax import lax
from jax.experimental import pallas as pl
from jax.experimental.pallas import tpu as pltpu
from jax.sharding import PartitionSpec as P

GY = 4
TICKS = 6
PIECES = 4
VMEM = 51 << 20
LATE = 1 << 20
FIRST = (
    (0, 61, 75, 201, 15, 143, 172, 368, 150, 221, 240, 212, 130, 288, 293, 377),
    (514, 309, 112, 148, 589, 141, 112, 119, 421, 85, 79, 5, 98, 44, 29, 0),
)
EVERY = (
    (0, 234, 218, 74, 107, 436, 428, 186, 137, 335, 359, 412, 30, 535, 528, 664),
    (386, 206, 470, 156, 275, 438, 434, 272, 88, 382, 384, 183, 363, 103, 123, 0),
)
COLS = 256
MESH = pl.DeviceIdType.MESH
NT = (((1,), (1,)), ((), ()))
NN = (((1,), (0,)), ((), ()))


def dot(a, b, dims):
    return lax.dot_general(a, b, dims, preferred_element_type=jnp.float32)


def sweep(
    count,
    freqs,
    subs,
    trace_hbm,
    interior_hbm,
    fired_hbm,
    heard_hbm,
    shot_ref,
    left_hbm,
    right_hbm,
    trace,
    interior,
    bank,
    plain,
    src_ref,
    val,
    recv,
    xin,
    wave,
    back,
    load_sem,
    bank_sem,
    send_sem,
    recv_sem,
    hand_sem,
    swap_send,
    swap_recv,
    keep_sem,
):
    total = count * subs
    rows = total // GY
    deepest = rows - 1 + GY - 1
    spare = max(0, deepest - TICKS)
    reach = GY // subs
    chunks = freqs * PIECES
    width = val.shape[-1]
    tall = val.shape[-2]
    half = tall // 2
    me = lax.axis_index("sub")
    q = lax.axis_index("freq")
    other = 1 - q

    def place(l):
        g = lax.rem(me * subs + l + GY + 1, total)
        return g // GY, lax.rem(g, GY)

    def depth(l, way):
        r, c = place(l)
        return r + c if way == 0 else deepest - r - c

    def bank_load(way, l, f):
        hbm = (fired_hbm, heard_hbm)[way]
        return pltpu.make_async_copy(hbm.at[f, l], bank.at[way, l, f], bank_sem.at[way, l, f])

    def map_load(m, f, l):
        hbm, vmem = ((trace_hbm, trace), (interior_hbm, interior))[m]
        return pltpu.make_async_copy(hbm.at[f, l], vmem.at[f, l], load_sem.at[m, f, l])

    every = [(f, l) for f in range(freqs) for l in range(subs)]
    fronts = [(l, way) for l in range(subs) for way in range(2)]

    def early(l, way):
        return depth(l, way) <= spare

    source = functools.reduce(jnp.logical_or, [early(l, way) for l, way in fronts])

    def load_rest():
        for f in range(freqs):
            for l, way in fronts:

                @pl.when(jnp.logical_not(early(l, way)))
                def _():
                    bank_load(way, l, f).start()

        for f, l in every:
            map_load(0, f, l).start()

    for f in range(freqs):
        for l, way in fronts:

            @pl.when(early(l, way))
            def _():
                bank_load(way, l, f).start()

    @pl.when(jnp.logical_not(source))
    def _():
        load_rest()

    barrier = pltpu.get_barrier_semaphore()
    for by in (1, count - 1, reach, count - reach):
        pl.semaphore_signal(
            barrier, inc=1, device_id={"sub": lax.rem(me + by, count)}, device_id_type=MESH
        )
    pl.semaphore_signal(barrier, inc=1, device_id={"freq": other}, device_id_type=MESH)

    def copy_of(ref, way, slot, v, ch, by, sem=None):
        return pltpu.make_async_remote_copy(
            src_ref=ref,
            dst_ref=recv.at[way, slot, v, ch],
            send_sem=send_sem.at[way, slot, v, ch] if sem is None else sem,
            recv_sem=recv_sem.at[way, slot, v, ch],
            device_id={"sub": lax.rem(me + (by if way == 0 else count - by), count)},
            device_id_type=MESH,
        )

    def edges(l, way):
        r, c = place(l)
        if way == 0:
            return r > 0, c > 0, r < rows - 1, c < GY - 1, l == 0, l == subs - 1, l - 1
        return r < rows - 1, c < GY - 1, r > 0, c > 0, l == subs - 1, l == 0, l + 1

    relays = reach == 2 and count % 2 == 0
    parity = lax.rem(me, 2)

    def both(*flags):
        return functools.reduce(jnp.logical_and, flags)

    def send(ref, l, way, v, ch):
        _, _, below, aside, _, far_out, _ = edges(l, way)

        @pl.when(below)
        def _():
            copy_of(ref, way, 1 + l, v, ch, reach).start()

        if far_out:

            @pl.when(direct(way, aside, below))
            def _():
                copy_of(ref, way, 0, v, ch, 1).start()

    def direct(way, aside, below):
        if not relays:
            return aside
        return both(aside, jnp.logical_not(both(parity == 1 - way, below)))

    def handed(l, way):
        above, _, _, _, _, far_out, _ = edges(l, way)
        return both(parity == 1 - way, above) if relays and far_out else None

    def hand_on(way, l, v, ch):
        return copy_of(
            recv.at[way, 1 + l, v, ch], way, 0, v, ch, count - 1, sem=hand_sem.at[way, v, ch]
        )

    def each(body):
        if spare == 0:
            lax.fori_loop(0, chunks, lambda ch, _: (body(0, ch), 0)[1], 0)
        else:

            def outer(v, _):
                lax.fori_loop(0, chunks, lambda ch, _: (body(v, ch), 0)[1], 0)
                return 0

            lax.fori_loop(0, spare + 1, outer, 0)

    shots = shot_ref.shape[1]
    number = lax.broadcasted_iota(jnp.int32, (bank.shape[-1], shots), 0)
    chooser = jnp.transpose((number == shot_ref[...]).astype(jnp.float32)).astype(jnp.bfloat16)

    def pick(way, l, f):
        bank_load(way, l, f).wait()
        plain[...] = bank[way, l, f].astype(jnp.float32)
        for c in range(2):
            rows_of = plain[pl.ds(c, width, stride=2), :].astype(jnp.bfloat16)
            picked = dot(chooser, rows_of, NT).astype(jnp.bfloat16)
            for piece in range(PIECES):
                src_ref[way, l, f * PIECES + piece, c * half : (c + 1) * half, :] = picked[
                    piece * half : (piece + 1) * half
                ]

    def first(v, ch):
        for l, way in fronts:

            @pl.when(depth(l, way) == v)
            def _():
                send(src_ref.at[way, l, ch], l, way, v, ch)
                val[way, l, v, ch] = src_ref[way, l, ch]

    def begin(f, _):
        for l, way in fronts:

            @pl.when(early(l, way))
            def _():
                pick(way, l, f)

        @pl.when(f == 0)
        def _():
            pl.semaphore_wait(barrier, 5)

        for v in range(spare + 1):
            lax.fori_loop(
                f * PIECES, (f + 1) * PIECES, lambda ch, _: (first(v, ch), 0)[1], 0
            )
        return 0

    lax.fori_loop(0, freqs, begin, 0)

    @pl.when(source)
    def _():
        load_rest()

    for l, way in fronts:

        @pl.when(jnp.logical_not(early(l, way)))
        def _():
            for f in range(freqs if spare else 1):
                pick(way, l, f)

    for f, l in every:
        map_load(0, f, l).wait()
    for f, l in every:
        map_load(1, f, l).start()

    def step(t, v, ch, l, way):
        f = ch // PIECES
        above, beside, _, _, far_in, _, near = edges(l, way)

        @pl.when(above)
        def _():
            copy_of(val.at[way, l, v, ch], way, 1 + l, v, ch, reach).wait_recv()
            hands = handed(l, way)
            if hands is not None:

                @pl.when(hands)
                def _():
                    hand_on(way, l, v, ch).start()

            xin[...] = recv[way, 1 + l, v, ch]

        @pl.when(jnp.logical_not(above))
        def _():
            xin[...] = jnp.zeros_like(xin)

        @pl.when(beside)
        def _():
            if far_in:
                copy_of(val.at[way, l, v, ch], way, 0, v, ch, 1).wait_recv()
                side = recv[way, 0, v, ch]
            else:
                side = val[way, near, v, ch]
            xin[...] = (xin[...].astype(jnp.float32) + side.astype(jnp.float32)).astype(
                jnp.bfloat16
            )

        x = xin[...]
        for n in range(0, width, COLS):
            span = slice(n, n + COLS)
            if way == 0:
                p = dot(x, trace[f, l, 0, span, :], NT)
                s = dot(x, trace[f, l, 1, span, :], NT)
                real, imag = p[:half] - s[half:], p[half:] + s[:half]
            else:
                p = dot(x, trace[f, l, 0, :, span], NN)
                s = dot(x, trace[f, l, 1, :, span], NN)
                real, imag = p[:half] + s[half:], p[half:] - s[:half]
            mine = src_ref[way, l, ch, :, span].astype(jnp.float32)
            val[way, l, v, ch, :half, span] = (mine[:half] + real).astype(jnp.bfloat16)
            val[way, l, v, ch, half:, span] = (mine[half:] + imag).astype(jnp.bfloat16)

        @pl.when(t < TICKS)
        def _():
            send(val.at[way, l, v, ch], l, way, v, ch)

        if spare == 0:

            @pl.when(both(lax.rem(ch, PIECES) == PIECES - 2, f + 1 < freqs))
            def _():
                pick(way, l, f + 1)

    width_half = width // 2
    keep = pl.ds(pl.multiple_of(q * width_half, width_half), width_half)
    give = pl.ds(pl.multiple_of(other * width_half, width_half), width_half)

    def swaps(l, f):
        for k, (src, dst) in enumerate(
            (
                (wave.at[l, f, :, give], left_hbm.at[l, freqs + f]),
                (back.at[l, f], right_hbm.at[l, freqs + f]),
            )
        ):
            yield pltpu.make_async_remote_copy(
                src_ref=src,
                dst_ref=dst,
                send_sem=swap_send.at[k, l, f],
                recv_sem=swap_recv.at[k, l, f],
                device_id={"freq": other},
                device_id_type=MESH,
            )

    def keeps(l, f):
        for k, (src, dst) in enumerate(
            (
                (wave.at[l, f, :, keep], left_hbm.at[l, f]),
                (back.at[l, f], right_hbm.at[l, f]),
            )
        ):
            yield pltpu.make_async_copy(src, dst, keep_sem.at[k, l, f])

    def inside(l, f):
        map_load(1, f, l).wait()
        stack = []
        for way in range(2):
            v = 0 if spare == 0 else jnp.maximum(depth(l, way) - TICKS, 0)
            for piece in range(PIECES):
                stack.append(val[way, l, v, f * PIECES + piece])
        x = jnp.concatenate(stack, axis=0)
        high = x.shape[0] // 2
        for n in range(0, width, COLS):
            span = slice(n, n + COLS)
            p = dot(x, interior[f, l, 0, span, :], NT)
            s = dot(x, interior[f, l, 1, span, :], NT)
            p = p.reshape(-1, 2, half, COLS)
            s = s.reshape(-1, 2, half, COLS)
            y = jnp.stack([p[:, 0] - s[:, 1], p[:, 1] + s[:, 0]], axis=1)
            y = y.reshape(2, high, COLS).astype(jnp.bfloat16)
            wave[l, f, :, span] = y[0]
            back[l, f, :, span] = y[1]
        for copy in (*swaps(l, f), *keeps(l, f)):
            copy.start()

    kinds = []
    for l in range(subs):
        for way in range(2):
            r, c = place(l)
            for v in range(spare + 1):
                t = depth(l, way) - v
                begin, pace = 60 * t, 300
                if (count, total, spare) == (8, 16, 0):
                    for g in range(total):
                        here = r * GY + c == g
                        begin = jnp.where(here, FIRST[way][g], begin)
                        pace = jnp.where(here, EVERY[way][g], pace)
                kinds.append((l, way, v, t, both(t >= 1, t <= TICKS), begin * 10, pace))
    jobs = chunks * sum(valid.astype(jnp.int32) for *_, valid, _, _ in kinds)

    def corner(l):
        return jnp.logical_or(depth(l, 0) == 0, depth(l, 1) == 0)

    def turn(_, done):
        due = [
            jnp.where(both(valid, n < chunks), begin + pace * n, LATE)
            for n, (*_, valid, begin, pace) in zip(done, kinds)
        ]
        least = functools.reduce(jnp.minimum, due)
        free = jnp.bool_(True)
        after = []
        for n, time, (l, way, v, t, *_) in zip(done, due, kinds):
            mine = both(free, time == least)
            free = both(free, jnp.logical_not(mine))

            @pl.when(mine)
            def _():
                step(t, v, n, l, way)
                if spare == 0:

                    @pl.when(both(corner(l), lax.rem(n, PIECES) == PIECES - 1))
                    def _():
                        inside(l, n // PIECES)

            after.append(n + mine.astype(jnp.int32))
        return tuple(after)

    lax.fori_loop(0, jobs, turn, tuple(jnp.int32(0) for _ in kinds))

    for l in range(subs):

        @pl.when(jnp.logical_not(corner(l)) if spare == 0 else l >= 0)
        def _():
            lax.fori_loop(0, freqs, lambda f, _: (inside(l, f), 0)[1], 0)

    def finish(v, ch):
        for l in range(subs):
            for way in range(2):
                here = depth(l, way)
                _, _, below, aside, _, far_out, _ = edges(l, way)
                sent = jnp.logical_and(here >= v, here < v + TICKS)
                if far_out:

                    @pl.when(both(sent, direct(way, aside, below)))
                    def _():
                        copy_of(val.at[way, l, v, ch], way, 0, v, ch, 1).wait_send()

                hands = handed(l, way)
                if hands is not None:

                    @pl.when(both(hands, here - v >= 1, here - v <= TICKS))
                    def _():
                        hand_on(way, l, v, ch).wait_send()

                @pl.when(jnp.logical_and(sent, below))
                def _():
                    copy_of(val.at[way, l, v, ch], way, 1 + l, v, ch, reach).wait_send()

    each(finish)
    for f, l in every:
        for copy in (*swaps(l, f), *keeps(l, f)):
            copy.wait()


def per_device(trace_map, interior_map, excitation, receiver_data, shot_index):
    freqs, subs, _, width, _ = trace_map.shape
    shots = shot_index.shape[0]
    bank = excitation.shape[4]
    count = lax.axis_size("sub")
    half = shots // PIECES
    chunks = freqs * PIECES
    rows = count * subs // GY
    spare = max(0, rows + GY - 2 - TICKS)
    scale = (2.0 * shots * freqs * lax.axis_size("freq")) ** (-0.5)
    bf = jnp.bfloat16
    flat = (freqs, subs, 2 * width, bank)
    dma = pltpu.SemaphoreType.DMA
    front = (chunks, 2 * half, width)
    left, right = pl.pallas_call(
        functools.partial(sweep, count, freqs, subs),
        out_shape=[
            jax.ShapeDtypeStruct((subs, 2 * freqs, 2 * shots, width // 2), bf),
            jax.ShapeDtypeStruct((subs, 2 * freqs, 2 * shots, width), bf),
        ],
        in_specs=[pl.BlockSpec(memory_space=pltpu.HBM)] * 4
        + [pl.BlockSpec(memory_space=pltpu.VMEM)],
        out_specs=[pl.BlockSpec(memory_space=pl.ANY)] * 2,
        scratch_shapes=[
            pltpu.VMEM(trace_map.shape, bf),
            pltpu.VMEM(interior_map.shape, bf),
            pltpu.VMEM((2, subs, freqs, 2 * width, bank), bf),
            pltpu.VMEM((2 * width, bank), jnp.float32),
            pltpu.VMEM((2, subs) + front, bf),
            pltpu.VMEM((2, subs, spare + 1) + front, bf),
            pltpu.VMEM((2, subs + 1, spare + 1) + front, bf),
            pltpu.VMEM((2 * half, width), bf),
            pltpu.VMEM((subs, freqs, 2 * shots, width), bf),
            pltpu.VMEM((subs, freqs, 2 * shots, width), bf),
            dma((2, freqs, subs)),
            dma((2, subs, freqs)),
            dma((2, subs + 1, spare + 1, chunks)),
            dma((2, subs + 1, spare + 1, chunks)),
            dma((2, spare + 1, chunks)),
            dma((2, subs, freqs)),
            dma((2, subs, freqs)),
            dma((2, subs, freqs)),
        ],
        compiler_params=pltpu.CompilerParams(
            collective_id=0, has_side_effects=True, vmem_limit_bytes=VMEM
        ),
    )(
        trace_map,
        interior_map,
        excitation.reshape(flat),
        receiver_data.reshape(flat),
        shot_index.reshape(1, shots),
    )
    image = jnp.einsum("sfma,sfmc->sac", left, right, preferred_element_type=jnp.float32)
    return image * scale


def solution(mesh):
    placed = (
        P("freq", ("survey", "sub"), None, None, None),
        P("freq", ("survey", "sub"), None, None, None),
        P("freq", ("survey", "sub"), None, None, None),
        P("freq", ("survey", "sub"), None, None, None),
        P("survey"),
    )
    return jax.shard_map(
        per_device,
        mesh=mesh,
        in_specs=placed,
        out_specs=P(("survey", "sub"), "freq", None),
        check_vma=False,
    )
```

```python
import functools

import jax
import jax.numpy as jnp
from jax import lax
from jax.experimental import pallas as pl
from jax.experimental.pallas import tpu as pltpu
from jax.sharding import PartitionSpec as P

GY = 4
TICKS = 6
PIECES = 4
VMEM = 51 << 20
LATE = 1 << 20
FIRST = (
    (0, 61, 75, 201, 15, 143, 172, 368, 150, 221, 240, 212, 130, 288, 293, 377),
    (514, 309, 112, 148, 589, 141, 112, 119, 421, 85, 79, 5, 98, 44, 29, 0),
)
EVERY = (
    (0, 234, 218, 74, 107, 436, 428, 186, 137, 335, 359, 412, 30, 535, 528, 664),
    (386, 206, 470, 156, 275, 438, 434, 272, 88, 382, 384, 183, 363, 103, 123, 0),
)
COLS = 256
WIDE = 768
MESH = pl.DeviceIdType.MESH
NT = (((1,), (1,)), ((), ()))
NN = (((1,), (0,)), ((), ()))


def dot(a, b, dims):
    return lax.dot_general(a, b, dims, preferred_element_type=jnp.float32)


def sweep(
    count,
    freqs,
    subs,
    trace_hbm,
    interior_hbm,
    fired_hbm,
    heard_hbm,
    shot_ref,
    left_hbm,
    right_hbm,
    trace,
    interior,
    bank,
    plain,
    src_ref,
    val,
    recv,
    xin,
    wave,
    back,
    load_sem,
    bank_sem,
    send_sem,
    recv_sem,
    hand_sem,
    swap_send,
    swap_recv,
    keep_sem,
):
    total = count * subs
    rows = total // GY
    deepest = rows - 1 + GY - 1
    spare = max(0, deepest - TICKS)
    reach = GY // subs
    chunks = freqs * PIECES
    width = val.shape[-1]
    tall = val.shape[-2]
    half = tall // 2
    me = lax.axis_index("sub")
    q = lax.axis_index("freq")
    other = 1 - q

    def place(l):
        g = lax.rem(me * subs + l + GY + 1, total)
        return g // GY, lax.rem(g, GY)

    def depth(l, way):
        r, c = place(l)
        return r + c if way == 0 else deepest - r - c

    def bank_load(way, l, f):
        hbm = (fired_hbm, heard_hbm)[way]
        return pltpu.make_async_copy(hbm.at[f, l], bank.at[way, l, f], bank_sem.at[way, l, f])

    def map_load(m, f, l):
        hbm, vmem = ((trace_hbm, trace), (interior_hbm, interior))[m]
        return pltpu.make_async_copy(hbm.at[f, l], vmem.at[f, l], load_sem.at[m, f, l])

    every = [(f, l) for f in range(freqs) for l in range(subs)]
    fronts = [(l, way) for l in range(subs) for way in range(2)]

    def early(l, way):
        return depth(l, way) <= spare

    source = functools.reduce(jnp.logical_or, [early(l, way) for l, way in fronts])

    def load_rest():
        for f in range(freqs):
            for l, way in fronts:

                @pl.when(jnp.logical_not(early(l, way)))
                def _():
                    bank_load(way, l, f).start()

        for f, l in every:
            map_load(0, f, l).start()

    for f in range(freqs):
        for l, way in fronts:

            @pl.when(early(l, way))
            def _():
                bank_load(way, l, f).start()

    @pl.when(jnp.logical_not(source))
    def _():
        load_rest()

    barrier = pltpu.get_barrier_semaphore()
    for by in (1, count - 1, reach, count - reach):
        pl.semaphore_signal(
            barrier, inc=1, device_id={"sub": lax.rem(me + by, count)}, device_id_type=MESH
        )
    pl.semaphore_signal(barrier, inc=1, device_id={"freq": other}, device_id_type=MESH)

    def copy_of(ref, way, slot, v, ch, by, sem=None):
        return pltpu.make_async_remote_copy(
            src_ref=ref,
            dst_ref=recv.at[way, slot, v, ch],
            send_sem=send_sem.at[way, slot, v, ch] if sem is None else sem,
            recv_sem=recv_sem.at[way, slot, v, ch],
            device_id={"sub": lax.rem(me + (by if way == 0 else count - by), count)},
            device_id_type=MESH,
        )

    def edges(l, way):
        r, c = place(l)
        if way == 0:
            return r > 0, c > 0, r < rows - 1, c < GY - 1, l == 0, l == subs - 1, l - 1
        return r < rows - 1, c < GY - 1, r > 0, c > 0, l == subs - 1, l == 0, l + 1

    relays = reach == 2 and count % 2 == 0
    parity = lax.rem(me, 2)

    def both(*flags):
        return functools.reduce(jnp.logical_and, flags)

    def send(ref, l, way, v, ch):
        _, _, below, aside, _, far_out, _ = edges(l, way)

        if far_out:

            @pl.when(direct(way, aside, below))
            def _():
                copy_of(ref, way, 0, v, ch, 1).start()

        @pl.when(below)
        def _():
            copy_of(ref, way, 1 + l, v, ch, reach).start()

    def direct(way, aside, below):
        if not relays:
            return aside
        return both(aside, jnp.logical_not(both(parity == 1 - way, below)))

    def handed(l, way):
        above, _, _, _, _, far_out, _ = edges(l, way)
        return both(parity == 1 - way, above) if relays and far_out else None

    def hand_on(way, l, v, ch):
        return copy_of(
            recv.at[way, 1 + l, v, ch], way, 0, v, ch, count - 1, sem=hand_sem.at[way, v, ch]
        )

    def each(body):
        if spare == 0:
            lax.fori_loop(0, chunks, lambda ch, _: (body(0, ch), 0)[1], 0)
        else:

            def outer(v, _):
                lax.fori_loop(0, chunks, lambda ch, _: (body(v, ch), 0)[1], 0)
                return 0

            lax.fori_loop(0, spare + 1, outer, 0)

    shots = shot_ref.shape[1]
    number = lax.broadcasted_iota(jnp.int32, (bank.shape[-1], shots), 0)
    chooser = jnp.transpose((number == shot_ref[...]).astype(jnp.float32)).astype(jnp.bfloat16)

    def pick(way, l, f):
        bank_load(way, l, f).wait()
        plain[...] = bank[way, l, f].astype(jnp.float32)
        for c in range(2):
            rows_of = plain[pl.ds(c, width, stride=2), :].astype(jnp.bfloat16)
            picked = dot(chooser, rows_of, NT).astype(jnp.bfloat16)
            for piece in range(PIECES):
                src_ref[way, l, f * PIECES + piece, c * half : (c + 1) * half, :] = picked[
                    piece * half : (piece + 1) * half
                ]

    def first(v, ch):
        for l, way in fronts:

            @pl.when(depth(l, way) == v)
            def _():
                send(src_ref.at[way, l, ch], l, way, v, ch)
                val[way, l, v, ch] = src_ref[way, l, ch]

    def begin(f, _):
        for l, way in fronts:

            @pl.when(early(l, way))
            def _():
                pick(way, l, f)

        @pl.when(f == 0)
        def _():
            pl.semaphore_wait(barrier, 5)

        for v in range(spare + 1):
            lax.fori_loop(
                f * PIECES, (f + 1) * PIECES, lambda ch, _: (first(v, ch), 0)[1], 0
            )
        return 0

    lax.fori_loop(0, freqs, begin, 0)

    @pl.when(source)
    def _():
        load_rest()

    for l, way in fronts:

        @pl.when(jnp.logical_not(early(l, way)))
        def _():
            for f in range(freqs if spare else 1):
                pick(way, l, f)

    for f, l in every:
        map_load(0, f, l).wait()
    for f, l in every:
        map_load(1, f, l).start()

    def step(t, v, ch, l, way):
        f = ch // PIECES
        above, beside, _, _, far_in, _, near = edges(l, way)

        @pl.when(above)
        def _():
            copy_of(val.at[way, l, v, ch], way, 1 + l, v, ch, reach).wait_recv()
            hands = handed(l, way)
            if hands is not None:

                @pl.when(hands)
                def _():
                    hand_on(way, l, v, ch).start()

            xin[...] = recv[way, 1 + l, v, ch]

        @pl.when(jnp.logical_not(above))
        def _():
            xin[...] = jnp.zeros_like(xin)

        @pl.when(beside)
        def _():
            if far_in:
                copy_of(val.at[way, l, v, ch], way, 0, v, ch, 1).wait_recv()
                side = recv[way, 0, v, ch]
            else:
                side = val[way, near, v, ch]
            xin[...] = (xin[...].astype(jnp.float32) + side.astype(jnp.float32)).astype(
                jnp.bfloat16
            )

        x = xin[...]
        for n in range(0, width, WIDE):
            span = slice(n, n + WIDE)
            if way == 0:
                p = dot(x, trace[f, l, 0, span, :], NT)
                s = dot(x, trace[f, l, 1, span, :], NT)
                real, imag = p[:half] - s[half:], p[half:] + s[:half]
            else:
                p = dot(x, trace[f, l, 0, :, span], NN)
                s = dot(x, trace[f, l, 1, :, span], NN)
                real, imag = p[:half] + s[half:], p[half:] - s[:half]
            mine = src_ref[way, l, ch, :, span].astype(jnp.float32)
            val[way, l, v, ch, :half, span] = (mine[:half] + real).astype(jnp.bfloat16)
            val[way, l, v, ch, half:, span] = (mine[half:] + imag).astype(jnp.bfloat16)

        @pl.when(t < TICKS)
        def _():
            send(val.at[way, l, v, ch], l, way, v, ch)

        if spare == 0:

            @pl.when(both(lax.rem(ch, PIECES) == PIECES - 2, f + 1 < freqs))
            def _():
                pick(way, l, f + 1)

    width_half = width // 2
    keep = pl.ds(pl.multiple_of(q * width_half, width_half), width_half)
    give = pl.ds(pl.multiple_of(other * width_half, width_half), width_half)

    def swaps(l, f):
        for k, (src, dst) in enumerate(
            (
                (wave.at[l, f, :, give], left_hbm.at[l, freqs + f]),
                (back.at[l, f], right_hbm.at[l, freqs + f]),
            )
        ):
            yield pltpu.make_async_remote_copy(
                src_ref=src,
                dst_ref=dst,
                send_sem=swap_send.at[k, l, f],
                recv_sem=swap_recv.at[k, l, f],
                device_id={"freq": other},
                device_id_type=MESH,
            )

    def keeps(l, f):
        for k, (src, dst) in enumerate(
            (
                (wave.at[l, f, :, keep], left_hbm.at[l, f]),
                (back.at[l, f], right_hbm.at[l, f]),
            )
        ):
            yield pltpu.make_async_copy(src, dst, keep_sem.at[k, l, f])

    def inside(l, f):
        map_load(1, f, l).wait()
        stack = []
        for way in range(2):
            v = 0 if spare == 0 else jnp.maximum(depth(l, way) - TICKS, 0)
            for piece in range(PIECES):
                stack.append(val[way, l, v, f * PIECES + piece])
        x = jnp.concatenate(stack, axis=0)
        high = x.shape[0] // 2
        for n in range(0, width, COLS):
            span = slice(n, n + COLS)
            p = dot(x, interior[f, l, 0, span, :], NT)
            s = dot(x, interior[f, l, 1, span, :], NT)
            p = p.reshape(-1, 2, half, COLS)
            s = s.reshape(-1, 2, half, COLS)
            y = jnp.stack([p[:, 0] - s[:, 1], p[:, 1] + s[:, 0]], axis=1)
            y = y.reshape(2, high, COLS).astype(jnp.bfloat16)
            wave[l, f, :, span] = y[0]
            back[l, f, :, span] = y[1]
        for copy in (*swaps(l, f), *keeps(l, f)):
            copy.start()

    kinds = []
    for l in range(subs):
        for way in range(2):
            r, c = place(l)
            for v in range(spare + 1):
                t = depth(l, way) - v
                begin, pace = 60 * t, 300
                if (count, total, spare) == (8, 16, 0):
                    for g in range(total):
                        here = r * GY + c == g
                        begin = jnp.where(here, FIRST[way][g], begin)
                        pace = jnp.where(here, EVERY[way][g], pace)
                kinds.append((l, way, v, t, both(t >= 1, t <= TICKS), begin * 10, pace))
    jobs = chunks * sum(valid.astype(jnp.int32) for *_, valid, _, _ in kinds)

    def corner(l):
        return jnp.logical_or(depth(l, 0) == 0, depth(l, 1) == 0)

    def turn(_, done):
        due = [
            jnp.where(both(valid, n < chunks), begin + pace * n, LATE)
            for n, (*_, valid, begin, pace) in zip(done, kinds)
        ]
        least = functools.reduce(jnp.minimum, due)
        free = jnp.bool_(True)
        after = []
        for n, time, (l, way, v, t, *_) in zip(done, due, kinds):
            mine = both(free, time == least)
            free = both(free, jnp.logical_not(mine))

            @pl.when(mine)
            def _():
                step(t, v, n, l, way)
                if spare == 0:

                    @pl.when(both(corner(l), lax.rem(n, PIECES) == PIECES - 1))
                    def _():
                        inside(l, n // PIECES)

            after.append(n + mine.astype(jnp.int32))
        return tuple(after)

    lax.fori_loop(0, jobs, turn, tuple(jnp.int32(0) for _ in kinds))

    for l in range(subs):

        @pl.when(jnp.logical_not(corner(l)) if spare == 0 else l >= 0)
        def _():
            lax.fori_loop(0, freqs, lambda f, _: (inside(l, f), 0)[1], 0)

    def finish(v, ch):
        for l in range(subs):
            for way in range(2):
                here = depth(l, way)
                _, _, below, aside, _, far_out, _ = edges(l, way)
                sent = jnp.logical_and(here >= v, here < v + TICKS)
                if far_out:

                    @pl.when(both(sent, direct(way, aside, below)))
                    def _():
                        copy_of(val.at[way, l, v, ch], way, 0, v, ch, 1).wait_send()

                hands = handed(l, way)
                if hands is not None:

                    @pl.when(both(hands, here - v >= 1, here - v <= TICKS))
                    def _():
                        hand_on(way, l, v, ch).wait_send()

                @pl.when(jnp.logical_and(sent, below))
                def _():
                    copy_of(val.at[way, l, v, ch], way, 1 + l, v, ch, reach).wait_send()

    each(finish)
    for f, l in every:
        for copy in (*swaps(l, f), *keeps(l, f)):
            copy.wait()


def per_device(trace_map, interior_map, excitation, receiver_data, shot_index):
    freqs, subs, _, width, _ = trace_map.shape
    shots = shot_index.shape[0]
    bank = excitation.shape[4]
    count = lax.axis_size("sub")
    half = shots // PIECES
    chunks = freqs * PIECES
    rows = count * subs // GY
    spare = max(0, rows + GY - 2 - TICKS)
    scale = (2.0 * shots * freqs * lax.axis_size("freq")) ** (-0.5)
    bf = jnp.bfloat16
    flat = (freqs, subs, 2 * width, bank)
    dma = pltpu.SemaphoreType.DMA
    front = (chunks, 2 * half, width)
    left, right = pl.pallas_call(
        functools.partial(sweep, count, freqs, subs),
        out_shape=[
            jax.ShapeDtypeStruct((subs, 2 * freqs, 2 * shots, width // 2), bf),
            jax.ShapeDtypeStruct((subs, 2 * freqs, 2 * shots, width), bf),
        ],
        in_specs=[pl.BlockSpec(memory_space=pltpu.HBM)] * 4
        + [pl.BlockSpec(memory_space=pltpu.VMEM)],
        out_specs=[pl.BlockSpec(memory_space=pl.ANY)] * 2,
        scratch_shapes=[
            pltpu.VMEM(trace_map.shape, bf),
            pltpu.VMEM(interior_map.shape, bf),
            pltpu.VMEM((2, subs, freqs, 2 * width, bank), bf),
            pltpu.VMEM((2 * width, bank), jnp.float32),
            pltpu.VMEM((2, subs) + front, bf),
            pltpu.VMEM((2, subs, spare + 1) + front, bf),
            pltpu.VMEM((2, subs + 1, spare + 1) + front, bf),
            pltpu.VMEM((2 * half, width), bf),
            pltpu.VMEM((subs, freqs, 2 * shots, width), bf),
            pltpu.VMEM((subs, freqs, 2 * shots, width), bf),
            dma((2, freqs, subs)),
            dma((2, subs, freqs)),
            dma((2, subs + 1, spare + 1, chunks)),
            dma((2, subs + 1, spare + 1, chunks)),
            dma((2, spare + 1, chunks)),
            dma((2, subs, freqs)),
            dma((2, subs, freqs)),
            dma((2, subs, freqs)),
        ],
        compiler_params=pltpu.CompilerParams(
            collective_id=0, has_side_effects=True, vmem_limit_bytes=VMEM
        ),
    )(
        trace_map,
        interior_map,
        excitation.reshape(flat),
        receiver_data.reshape(flat),
        shot_index.reshape(1, shots),
    )
    image = jnp.einsum("sfma,sfmc->sac", left, right, preferred_element_type=jnp.float32)
    return image * scale


def solution(mesh):
    placed = (
        P("freq", ("survey", "sub"), None, None, None),
        P("freq", ("survey", "sub"), None, None, None),
        P("freq", ("survey", "sub"), None, None, None),
        P("freq", ("survey", "sub"), None, None, None),
        P("survey"),
    )
    return jax.shard_map(
        per_device,
        mesh=mesh,
        in_specs=placed,
        out_specs=P(("survey", "sub"), "freq", None),
        check_vma=False,
    )
```
